1024 devices in a mesh: slab: 32 (over x, y, core), group: 32 (over z).
Axes of the slice: x: 4, y: 4, z: 32, core: 2. Of those that a mesh axis runs over, the one named last changes fastest.
Arguments:
- grads: bfloat16 [256, 2048, 512], P('group', 'slab'), may hold values from -64 to 64
- grad_slot: int32 [32, 8], P('group'), may hold values from 0 to 7, each once within a row
- momentum: bfloat16 [256, 2048, 512], P('group', 'slab'), may hold values from -6 to 6
Outputs:
- new_momentum: bfloat16 [256, 2048, 512], P('group', 'slab')
- update: bfloat16 [256, 2048, 512], P('group', 'slab')
The draws below stay inside these ranges and needn't reach their ends.
All inputs are finite; a program needn't handle non-finite values.
Results may differ from the reference program's by a relative error of at most 0.0071.
Values may be sent and summed in bfloat16 or wider, within the bound.
A program may use at most 32 MiB of HBM per device.

```python
import jax
import jax.numpy as jnp
from jax import lax

M = 2048
K = 512
ITERS = 2
E_GRP = 8
EXPERTS = 256
N_GROUP = 32


def draw_grads(key, part):
    key_noise = jax.random.fold_in(key, 0)
    key_rough = jax.random.fold_in(key, 1)
    key_expert = jax.random.fold_in(key, 3)
    key_row = jax.random.fold_in(key, 4)
    expert_pos = jnp.arange(EXPERTS, dtype=jnp.float32) / max(EXPERTS - 1, 1)
    row_pos = jnp.arange(M, dtype=jnp.float32) / (M - 1)
    rough = jnp.exp(jax.random.uniform(key_rough, (EXPERTS, M, 1), minval=-0.5, maxval=0.5))
    expert_blocks = jnp.exp(jax.random.uniform(key_expert, (EXPERTS // E_GRP,), minval=-0.5, maxval=0.5))
    expert_level = jnp.repeat(expert_blocks, E_GRP, total_repeat_length=EXPERTS)
    row_blocks = jnp.exp(jax.random.uniform(key_row, (32,), minval=-0.5, maxval=0.5))
    row_level = jnp.repeat(row_blocks, M // 32, total_repeat_length=M)
    levels = expert_level[:, None, None] * row_level[None, :, None]
    spread = 0.6 * jnp.sqrt((1.0 + 2.0 * expert_pos)[:, None, None] * (1.0 + 2.0 * row_pos)[None, :, None]) * rough * levels
    values = jnp.clip(jax.random.normal(key_noise, (EXPERTS, M, K)), -4.0, 4.0) * spread
    return values.astype(jnp.bfloat16)


def block_levels(rng, shape, cuts, least, largest):
    gain, own = 1.0, jax.random.fold_in(rng, 6)
    for axis_at, blocks in cuts:
        steps = jnp.exp(jax.random.uniform(jax.random.fold_in(own, axis_at), (blocks,), jnp.float32, least / len(cuts), largest / len(cuts)))
        gain = gain * jnp.repeat(steps, shape[axis_at] // blocks).reshape([-1 if axis == axis_at else 1 for axis in range(len(shape))])
    return gain


def gaussian(stream_key, dims, width, bound, cuts=(), held_as=jnp.bfloat16):
    array = jax.random.normal(stream_key, dims, jnp.float32) * width
    if len(cuts) > 0:
        array = block_levels(stream_key, dims, cuts, -0.22, 0.18) * array
    return jnp.clip(array, min=-bound, max=bound).astype(held_as)


def setup_inputs(seed: int = 0) -> dict:
    arg_keys = jax.random.split(jax.random.key(seed), 4)
    grads = draw_grads(jax.random.fold_in(arg_keys[3], 71), 0)
    grad_slot = jax.vmap(lambda own: jax.random.permutation(own, E_GRP))(jax.random.split(arg_keys[1], N_GROUP)).reshape((N_GROUP, E_GRP)).astype(jnp.int32)
    momentum = gaussian(arg_keys[2], (EXPERTS, M, K), 1.0, 6.0, ((0, 32), (1, 32)))
    return dict(grads=grads, grad_slot=grad_slot, momentum=momentum)


COEF_A = 3.4445
COEF_B = -4.775
COEF_C = 2.0315
DECAY_RATE = 0.95

def newton_factor(current):
    identity = jnp.eye(K, dtype=jnp.float32)
    product = current
    for iteration in range(ITERS):
        rounded = current.astype(jnp.bfloat16)
        squared = jnp.dot(rounded, rounded, preferred_element_type=jnp.float32)
        poly = COEF_A * identity + COEF_B * current + COEF_C * squared
        poly_half = poly.astype(jnp.bfloat16)
        if iteration == 0:
            product = poly
        else:
            product = jnp.dot(product.astype(jnp.bfloat16), poly_half, preferred_element_type=jnp.float32)
        if iteration < ITERS - 1:
            halfway = jnp.dot(rounded, poly_half, preferred_element_type=jnp.float32).astype(jnp.bfloat16)
            current = jnp.dot(poly_half, halfway, preferred_element_type=jnp.float32)
    return product

def reference(grads, grad_slot, momentum):
    total_sq = jnp.sum(jnp.square(grads.astype(jnp.float32)))
    root_mean = jnp.sqrt(total_sq / (EXPERTS * M * K) + 1e-06)
    clip_factor = jnp.minimum(1.0, 1.0 / root_mean)
    source_rows = jnp.arange(EXPERTS, dtype=jnp.int32) // E_GRP * E_GRP + grad_slot.reshape(-1).astype(jnp.int32)

    def update_one(pair):
        source, moment = pair
        gradient = lax.dynamic_index_in_dim(grads, source, 0, keepdims=False)
        fresh = (DECAY_RATE * moment.astype(jnp.float32) + clip_factor * gradient.astype(jnp.float32)).astype(jnp.bfloat16)
        gram_matrix = lax.dot_general(fresh, fresh, (((0,), (0,)), ((), ())), preferred_element_type=jnp.float32)
        frobenius = jnp.trace(gram_matrix) + 1e-06
        product = newton_factor(gram_matrix / frobenius)
        scaled_q = (product / jnp.sqrt(frobenius)).astype(jnp.bfloat16)
        result = jnp.sqrt(jnp.float32(M)) * jnp.dot(fresh, scaled_q, preferred_element_type=jnp.float32)
        return (fresh, result.astype(jnp.bfloat16))
    new_momentum, update = lax.map(update_one, (source_rows, momentum))
    return (new_momentum, update)
```

```python
import jax
import jax.numpy as jnp
from jax import lax
from jax.experimental import pallas as pl
from jax.experimental.pallas import tpu as pltpu
from jax.sharding import PartitionSpec as P

MESH = pl.DeviceIdType.MESH

SIDE = 4
CORES = 2
SLABS = SIDE * SIDE * CORES
CHIPS = SIDE * SIDE
GROUPS = 32
EXPERTS = 8
ROWS = 64
M = SLABS * ROWS
K = 512
HALF = K // 2
OWN = CHIPS * ROWS
REACH = 4

COEF_A = 3.4445
COEF_B = -4.775
COEF_C = 2.0315
DECAY_RATE = 0.95
ENTRIES = GROUPS * EXPERTS * M * K

COLUMNS = (2, 1, 3, 0)
NEAR = tuple(off for off in range(-REACH, REACH) if off != 0)


def squares(block):
    wide = block.astype(jnp.float32)
    return jnp.sum((wide * wide).reshape(ROWS // 8, 8, K), axis=0)


def fresh(moment, gradient, factor):
    return (
        DECAY_RATE * moment.astype(jnp.float32) + factor * gradient.astype(jnp.float32)
    ).astype(jnp.bfloat16)


def dot(left, right):
    return jnp.dot(left, right, preferred_element_type=jnp.float32)


def kernel(
    slot_ref,
    grads_hbm,
    momentum_hbm,
    new_ref,
    update_ref,
    grads_in,
    pair,
    raw,
    own_new,
    part,
    slab_parts,
    plane,
    near_parts,
    window,
    window_parts,
    wide_window,
    wide_parts,
    far_parts,
    gram_own,
    gram_other,
    current,
    rounded,
    poly_first,
    halfway,
    poly_second,
    scaled,
    outgoing,
    load_sem,
    slab_send,
    slab_recv,
    near_send,
    near_recv,
    step_send,
    step_recv,
    raw_send,
    raw_recv,
    local_sem,
    gram_send,
    gram_recv,
    back_send,
    back_recv,
):
    slab = lax.axis_index("slab")
    group = lax.axis_index("group")
    chip = slab // CORES
    core = slab % CORES
    x = chip // SIDE
    y = chip % SIDE
    active = (x + y) % 2 == 0
    mine = x * 2 + y // 2

    def along_slab(other):
        return (other, group)

    def along_group(offset):
        return (slab, (group + offset + GROUPS) % GROUPS)

    def send(src, dst, send_sem, recv_sem, device):
        return pltpu.make_async_remote_copy(
            src_ref=src,
            dst_ref=dst,
            send_sem=send_sem,
            recv_sem=recv_sem,
            device_id=device,
            device_id_type=MESH,
        )

    load_grads = pltpu.make_async_copy(grads_hbm, grads_in, load_sem.at[0])
    load_momentum = pltpu.make_async_copy(momentum_hbm, pair.at[0], load_sem.at[1])
    load_grads.start()
    load_momentum.start()

    barrier = pltpu.get_barrier_semaphore()
    for offset in NEAR + (REACH,):
        pl.semaphore_signal(barrier, inc=1, device_id=along_group(offset), device_id_type=MESH)

    @pl.loop(1, SLABS)
    def _(step):
        pl.semaphore_signal(
            barrier, inc=1, device_id=along_slab((slab + step) % SLABS), device_id_type=MESH
        )

    load_grads.wait()
    total = jnp.zeros((8, K), jnp.float32)
    for expert in range(EXPERTS):
        block = grads_in[slot_ref[0, expert]]
        pair[1, expert] = block
        total += squares(block)
    lanes = total[:, :128] + total[:, 128:256] + total[:, 256:384] + total[:, 384:]
    part[...] = jnp.sum(lanes, axis=0, keepdims=True)
    load_momentum.wait()
    pl.semaphore_wait(barrier, SLABS - 1 + len(NEAR) + 1)

    def slab_copy(step):
        return send(
            part,
            slab_parts.at[step],
            slab_send.at[step],
            slab_recv.at[step],
            along_slab((slab + step) % SLABS),
        )

    @pl.loop(1, SLABS)
    def _(step):
        slab_copy(step).start()

    def raw_copies(hops, which):
        column = (x + hops) % SIDE
        expert = column * 2 + which
        row = which * 2 + column % 2
        place = ((x + SIDE - column) % SIDE) * SIDE + (y + SIDE - row) % SIDE
        target = (column * SIDE + row) * CORES + core
        index = COLUMNS.index(hops) * 2 + which
        return target, expert, [
            send(
                pair.at[kind, expert],
                raw.at[kind, place],
                raw_send.at[kind, index],
                raw_recv.at[kind, place],
                along_slab(target),
            )
            for kind in range(2)
        ]

    def local_copies(expert):
        return [
            pltpu.make_async_copy(pair.at[kind, expert], raw.at[kind, 0], local_sem.at[kind])
            for kind in range(2)
        ]

    for hops in COLUMNS:
        for which in range(2):
            target, expert, copies = raw_copies(hops, which)

            @pl.when(target != slab)
            def _():
                for copy in copies:
                    copy.start()

    @pl.when(active)
    def _():
        for copy in local_copies(mine):
            copy.start()

    @pl.loop(1, SLABS)
    def _(step):
        slab_copy(step).wait_recv()

    plane[...] = part[...] + jnp.sum(slab_parts[1:], axis=0)

    near_copies = [
        send(
            plane,
            near_parts.at[index],
            near_send.at[index],
            near_recv.at[index],
            along_group(offset),
        )
        for index, offset in enumerate(NEAR)
    ]

    def step_copies(src, dst, stage):
        return [
            send(
                src(side),
                dst.at[side],
                step_send.at[stage, side],
                step_recv.at[stage, side],
                along_group(offset),
            )
            for side, offset in enumerate((REACH, -REACH))
        ]

    window_copies = step_copies(lambda side: window, window_parts, 0)
    wide_copies = step_copies(lambda side: wide_window, wide_parts, 1)
    far_copies = step_copies(lambda side: wide_parts.at[side], far_parts, 2)

    for copy in near_copies:
        copy.start()
    for copy in near_copies:
        copy.wait_recv()
    window[...] = plane[...] + jnp.sum(near_parts[...], axis=0)
    for copy in window_copies:
        copy.start()
    for copy in window_copies:
        copy.wait_recv()
    wide_window[...] = jnp.sum(window_parts[...], axis=0)
    for copy in wide_copies:
        copy.start()
    for copy, forward in zip(wide_copies, far_copies):
        copy.wait_recv()
        forward.start()
    for copy in far_copies:
        copy.wait_recv()

    total_sq = jnp.sum(jnp.sum(far_parts[...], axis=0), axis=1, keepdims=True)
    root_mean = jnp.sqrt(total_sq / ENTRIES + 1e-06)
    factor = jnp.minimum(1.0, 1.0 / root_mean)

    def own_result():
        for expert in range(EXPERTS):
            new_ref[expert] = fresh(pair[0, expert], pair[1, expert], factor)

    def gram_copies():
        partner = along_slab(chip * CORES + 1 - core)
        return [
            send(
                gram_own.at[index],
                gram_other.at[index],
                gram_send.at[index],
                gram_recv.at[index],
                partner,
            )
            for index in range(3)
        ]

    def back_copy(hops_x, hops_y):
        place = hops_x * SIDE + hops_y
        target = ((x + hops_x) % SIDE * SIDE + (y + hops_y) % SIDE) * CORES + core
        return send(
            outgoing.at[place],
            update_ref.at[mine],
            back_send.at[place],
            back_recv.at[mine],
            along_slab(target),
        )

    @pl.when(active)
    def _():
        for copy in local_copies(mine):
            copy.wait()

        @pl.loop(1, CHIPS)
        def _(place):
            for kind in range(2):
                send(
                    pair.at[kind, 0],
                    raw.at[kind, place],
                    raw_send.at[kind, 0],
                    raw_recv.at[kind, place],
                    along_slab(slab),
                ).wait_recv()

        for place in range(CHIPS):
            own_new[place * ROWS : (place + 1) * ROWS, :] = fresh(
                raw[0, place], raw[1, place], factor
            )

        for index, (left, right) in enumerate(((0, 0), (0, 1), (1, 1))):
            gram_own[index] = lax.dot_general(
                own_new[:, left * HALF : (left + 1) * HALF],
                own_new[:, right * HALF : (right + 1) * HALF],
                (((0,), (0,)), ((), ())),
                preferred_element_type=jnp.float32,
            )
            if index > 0:
                gram_copies()[index - 1].start()
        gram_copies()[2].start()
        for copy in gram_copies():
            copy.wait_recv()

        trace = jnp.zeros((128, 128), jnp.float32)
        for index in (0, 2):
            whole = gram_own[index] + gram_other[index]
            gram_own_low, gram_own_high = whole[:128, :128], whole[128:, 128:]
            trace += gram_own_low + gram_own_high
        eye = lax.broadcasted_iota(jnp.int32, (128, 128), 0) == lax.broadcasted_iota(
            jnp.int32, (128, 128), 1
        )
        trace = jnp.where(eye, trace, 0.0)
        frobenius = (
            jnp.sum(jnp.sum(trace, axis=0, keepdims=True), axis=1, keepdims=True) + 1e-06
        )
        inverse = 1.0 / frobenius
        for index, (left, right) in enumerate(((0, 0), (0, 1), (1, 1))):
            block = (gram_own[index] + gram_other[index]) * inverse
            current[left * HALF : (left + 1) * HALF, right * HALF : (right + 1) * HALF] = block
            rounded[left * HALF : (left + 1) * HALF, right * HALF : (right + 1) * HALF] = (
                block.astype(jnp.bfloat16)
            )
            if index == 1:
                block = block.T
                current[HALF:, :HALF] = block
                rounded[HALF:, :HALF] = block.astype(jnp.bfloat16)

        def polynomial(into, start):
            rows = slice(start, start + HALF)
            squared = dot(rounded[rows, :], rounded[...])
            diagonal = lax.broadcasted_iota(jnp.int32, (HALF, K), 0) + start
            identity = jnp.where(
                diagonal == lax.broadcasted_iota(jnp.int32, (HALF, K), 1), COEF_A, 0.0
            )
            into[rows, :] = (identity + COEF_B * current[rows, :] + COEF_C * squared).astype(
                jnp.bfloat16
            )

        halves = (0, HALF)
        for start in halves:
            polynomial(poly_first, start)
        for start in halves:
            rows = slice(start, start + HALF)
            halfway[rows, :] = dot(rounded[rows, :], poly_first[...]).astype(jnp.bfloat16)
        for start in halves:
            rows = slice(start, start + HALF)
            following = dot(poly_first[rows, :], halfway[...])
            current[rows, :] = following
            rounded[rows, :] = following.astype(jnp.bfloat16)
        for start in halves:
            polynomial(poly_second, start)
        root = 1.0 / jnp.sqrt(frobenius)
        for start in halves:
            rows = slice(start, start + HALF)
            scaled[rows, :] = (dot(poly_first[rows, :], poly_second[...]) * root).astype(
                jnp.bfloat16
            )

        for turn, hops_x in enumerate(COLUMNS):
            start = hops_x * SIDE * ROWS
            result = jnp.sqrt(jnp.float32(M)) * dot(
                own_new[start : start + SIDE * ROWS, :], scaled[...]
            )
            outgoing[hops_x * SIDE : (hops_x + 1) * SIDE] = result.astype(jnp.bfloat16).reshape(
                SIDE, ROWS, K
            )
            if turn > 0:
                for hops_y in COLUMNS:
                    back_copy(COLUMNS[turn - 1], hops_y).start()
        for hops_y in COLUMNS[:-1]:
            back_copy(0, hops_y).start()
        update_ref[mine] = outgoing[0]

    own_result()

    for hops in COLUMNS:
        for which in range(2):
            target, expert, copies = raw_copies(hops, which)

            @pl.when(target != slab)
            def _():
                for copy in copies:
                    copy.wait_send()
                send(
                    outgoing.at[0],
                    update_ref.at[expert],
                    back_send.at[0],
                    back_recv.at[expert],
                    along_slab(target),
                ).wait_recv()

    @pl.when(active)
    def _():
        for copy in gram_copies():
            copy.wait_send()
        for hops_x in COLUMNS:
            for hops_y in COLUMNS:
                if (hops_x, hops_y) != (0, 0):
                    back_copy(hops_x, hops_y).wait_send()

    @pl.loop(1, SLABS)
    def _(step):
        slab_copy(step).wait_send()

    for copy in near_copies + window_copies + wide_copies + far_copies:
        copy.wait_send()


def on_device(grads, grad_slot, momentum):
    shape = jax.ShapeDtypeStruct(grads.shape, jnp.bfloat16)
    scalar = (1, 128)
    dma = pltpu.SemaphoreType.DMA
    return pl.pallas_call(
        kernel,
        out_shape=(shape, shape),
        in_specs=[
            pl.BlockSpec(memory_space=pltpu.SMEM),
            pl.BlockSpec(memory_space=pl.ANY),
            pl.BlockSpec(memory_space=pl.ANY),
        ],
        out_specs=(pl.BlockSpec(memory_space=pltpu.VMEM),) * 2,
        scratch_shapes=[
            pltpu.VMEM((EXPERTS, ROWS, K), jnp.bfloat16),
            pltpu.VMEM((2, EXPERTS, ROWS, K), jnp.bfloat16),
            pltpu.VMEM((2, CHIPS, ROWS, K), jnp.bfloat16),
            pltpu.VMEM((OWN, K), jnp.bfloat16),
            pltpu.VMEM(scalar, jnp.float32),
            pltpu.VMEM((SLABS, *scalar), jnp.float32),
            pltpu.VMEM(scalar, jnp.float32),
            pltpu.VMEM((len(NEAR), *scalar), jnp.float32),
            pltpu.VMEM(scalar, jnp.float32),
            pltpu.VMEM((2, *scalar), jnp.float32),
            pltpu.VMEM(scalar, jnp.float32),
            pltpu.VMEM((2, *scalar), jnp.float32),
            pltpu.VMEM((2, *scalar), jnp.float32),
            pltpu.VMEM((3, HALF, HALF), jnp.float32),
            pltpu.VMEM((3, HALF, HALF), jnp.float32),
            pltpu.VMEM((K, K), jnp.float32),
            pltpu.VMEM((K, K), jnp.bfloat16),
            pltpu.VMEM((K, K), jnp.bfloat16),
            pltpu.VMEM((K, K), jnp.bfloat16),
            pltpu.VMEM((K, K), jnp.bfloat16),
            pltpu.VMEM((K, K), jnp.bfloat16),
            pltpu.VMEM((CHIPS, ROWS, K), jnp.bfloat16),
            dma((2,)),
            dma((SLABS,)),
            dma((SLABS,)),
            dma((len(NEAR),)),
            dma((len(NEAR),)),
            dma((3, 2)),
            dma((3, 2)),
            dma((2, EXPERTS)),
            dma((2, CHIPS)),
            dma((2,)),
            dma((3,)),
            dma((3,)),
            dma((CHIPS,)),
            dma((EXPERTS,)),
        ],
        compiler_params=pltpu.CompilerParams(collective_id=0, has_side_effects=True),
        name="muon_step",
    )(grad_slot, grads, momentum)


def solution(mesh):
    in_specs = (P("group", "slab", None), P("group", None), P("group", "slab", None))
    out_specs = (P("group", "slab", None), P("group", "slab", None))
    return jax.shard_map(
        on_device, mesh=mesh, in_specs=in_specs, out_specs=out_specs, check_vma=False
    )
```

```python
import jax
import jax.numpy as jnp
from jax import lax
from jax.experimental import pallas as pl
from jax.experimental.pallas import tpu as pltpu
from jax.sharding import PartitionSpec as P

MESH = pl.DeviceIdType.MESH

SIDE = 4
CORES = 2
SLABS = SIDE * SIDE * CORES
CHIPS = SIDE * SIDE
GROUPS = 32
EXPERTS = 8
ROWS = 64
M = SLABS * ROWS
K = 512
HALF = K // 2
OWN = CHIPS * ROWS
REACH = 4

COEF_A = 3.4445
COEF_B = -4.775
COEF_C = 2.0315
DECAY_RATE = 0.95
ENTRIES = GROUPS * EXPERTS * M * K

COLUMNS = (2, 1, 3, 0)
BACK_RELAYED = ((2, 1), (2, 3), (1, 1), (3, 3))
NEAR = tuple(off for off in range(-REACH, REACH) if off != 0)


def squares(block):
    wide = block.astype(jnp.float32)
    return jnp.sum((wide * wide).reshape(ROWS // 8, 8, K), axis=0)


def fresh(moment, gradient, factor):
    return (
        DECAY_RATE * moment.astype(jnp.float32) + factor * gradient.astype(jnp.float32)
    ).astype(jnp.bfloat16)


def dot(left, right):
    return jnp.dot(left, right, preferred_element_type=jnp.float32)


def kernel(
    slot_hbm,
    grads_hbm,
    momentum_hbm,
    new_ref,
    update_ref,
    slot_ref,
    grads_in,
    pair,
    raw,
    relayed,
    back_relayed,
    own_new,
    part,
    slab_parts,
    plane,
    near_parts,
    window,
    window_parts,
    wide_window,
    far_parts,
    gram_own,
    gram_other,
    current,
    rounded,
    poly_first,
    halfway,
    poly_second,
    scaled,
    outgoing,
    load_sem,
    slab_send,
    slab_recv,
    near_send,
    near_recv,
    step_send,
    step_recv,
    raw_send,
    raw_recv,
    relay_send,
    relay_recv,
    local_sem,
    gram_send,
    gram_recv,
    back_send,
    back_recv,
    back_relay_send,
    back_relay_recv,
):
    slab = lax.axis_index("slab")
    group = lax.axis_index("group")
    chip = slab // CORES
    core = slab % CORES
    x = chip // SIDE
    y = chip % SIDE
    active = (x + y) % 2 == 0
    mine = x * 2 + y // 2

    def along_slab(other):
        return (other, group)

    def device_of(at_x, at_y):
        return (at_x * SIDE + at_y) * CORES + core

    def along_group(offset):
        return (slab, (group + offset + GROUPS) % GROUPS)

    def send(src, dst, send_sem, recv_sem, device):
        return pltpu.make_async_remote_copy(
            src_ref=src,
            dst_ref=dst,
            send_sem=send_sem,
            recv_sem=recv_sem,
            device_id=device,
            device_id_type=MESH,
        )

    load_grads = pltpu.make_async_copy(grads_hbm, grads_in, load_sem.at[0])
    load_momentum = pltpu.make_async_copy(momentum_hbm, pair.at[:, 0], load_sem.at[1])
    load_slots = pltpu.make_async_copy(slot_hbm, slot_ref, load_sem.at[2])
    load_slots.start()
    load_grads.start()
    load_momentum.start()

    barrier = pltpu.get_barrier_semaphore()
    for offset in NEAR + (REACH,):
        pl.semaphore_signal(barrier, inc=1, device_id=along_group(offset), device_id_type=MESH)

    @pl.loop(1, SLABS)
    def _(step):
        pl.semaphore_signal(
            barrier, inc=1, device_id=along_slab((slab + step) % SLABS), device_id_type=MESH
        )

    load_slots.wait()
    load_grads.wait()
    total = jnp.zeros((8, K), jnp.float32)
    for expert in range(EXPERTS):
        block = grads_in[slot_ref[0, expert]]
        pair[expert, 1] = block
        total += squares(block)
    lanes = total[:, :128] + total[:, 128:256] + total[:, 256:384] + total[:, 384:]
    part[...] = jnp.sum(lanes, axis=0, keepdims=True)
    load_momentum.wait()
    pl.semaphore_wait(barrier, SLABS - 1 + len(NEAR) + 1)

    def slab_copy(step):
        return send(
            part,
            slab_parts.at[step],
            slab_send.at[step],
            slab_recv.at[step],
            along_slab((slab + step) % SLABS),
        )

    @pl.loop(1, SLABS)
    def _(step):
        slab_copy(step).start()

    def raw_route(hops, which):
        column = (x + hops) % SIDE
        row = which * 2 + column % 2
        return (
            column * 2 + which,
            column,
            row,
            (SIDE - hops) % SIDE,
            (y + SIDE - row) % SIDE,
            COLUMNS.index(hops) * 2 + which,
        )

    def raw_direct(hops, which):
        expert, column, row, from_x, from_y, index = raw_route(hops, which)
        place = from_x * SIDE + from_y
        return send(
            pair.at[expert],
            raw.at[place],
            raw_send.at[index],
            raw_recv.at[place],
            along_slab(device_of(column, row)),
        )

    def raw_relayed(hops, which, slot, by_x, by_y):
        expert, column, row, from_x, from_y, index = raw_route(hops, which)
        return send(
            pair.at[expert],
            relayed.at[slot],
            raw_send.at[index],
            relay_recv.at[slot],
            along_slab(device_of((column + by_x) % SIDE, (row + by_y) % SIDE)),
        )

    def relay_forward(slot):
        if slot < 2:
            towards = (x, (y + 1 + 2 * (y % 2)) % SIDE)
            place = (1 + 2 * slot) * SIDE + 2
        else:
            towards = ((x + (3 if slot == 2 else 1)) % SIDE, y)
            place = 5 if slot == 2 else 15
        return send(
            relayed.at[slot],
            raw.at[place],
            relay_send.at[slot],
            raw_recv.at[place],
            along_slab(device_of(*towards)),
        )

    def relay_wait(slot):
        send(
            pair.at[0], relayed.at[slot], raw_send.at[0], relay_recv.at[slot], along_slab(slab)
        ).wait_recv()

    def relay(slots):
        @pl.when(jnp.logical_not(active))
        def _():
            for slot in slots:
                relay_wait(slot)
                relay_forward(slot).start()

    local_copy = pltpu.make_async_copy(pair.at[mine], raw.at[0], local_sem.at[0])

    @pl.loop(1, SLABS)
    def _(step):
        slab_copy(step).wait_recv()

    plane[...] = part[...] + jnp.sum(slab_parts[1:], axis=0)

    near_copies = [
        send(
            plane,
            near_parts.at[index],
            near_send.at[index],
            near_recv.at[index],
            along_group(offset),
        )
        for index, offset in enumerate(NEAR)
    ]

    def step_copies(src, dst, stage, reach):
        return [
            send(
                src,
                dst.at[side],
                step_send.at[stage, side],
                step_recv.at[stage, side],
                along_group(offset),
            )
            for side, offset in enumerate((reach, -reach))
        ]

    window_copies = step_copies(window, window_parts, 0, REACH)
    far_copies = step_copies(wide_window, far_parts, 1, 2 * REACH)

    for copy in near_copies:
        copy.start()

    for hops, diagonal in ((1, 3), (3, 1)):
        for which in range(2):
            from_y = raw_route(hops, which)[4]
            row = raw_route(hops, which)[2]

            @pl.when(from_y == diagonal)
            def _():
                raw_relayed(hops, which, 2 if diagonal == 1 else 3, SIDE - hops, 0).start()

            @pl.when(from_y == 2)
            def _():
                raw_relayed(
                    hops, which, 1 if diagonal == 3 else 0, 0, 1 + 2 * (row % 2)
                ).start()

    for hops in COLUMNS:
        for which in range(2):
            from_y = raw_route(hops, which)[4]
            if hops == 0:
                direct = from_y != 0
            elif hops == 2:
                direct = True
            else:
                direct = jnp.logical_and(from_y != 2, from_y != SIDE - hops)

            @pl.when(direct)
            def _():
                raw_direct(hops, which).start()

    @pl.when(active)
    def _():
        local_copy.start()

    for copy in near_copies:
        copy.wait_recv()
    window[...] = plane[...] + jnp.sum(near_parts[...], axis=0)
    for copy in window_copies:
        copy.start()
    relay((2, 3))
    for copy in window_copies:
        copy.wait_recv()
    wide_window[...] = jnp.sum(window_parts[...], axis=0)
    for copy in far_copies:
        copy.start()
    relay((0, 1))
    for copy in far_copies:
        copy.wait_recv()

    total_sq = jnp.sum(jnp.sum(far_parts[...], axis=0), axis=1, keepdims=True)
    root_mean = jnp.sqrt(total_sq / ENTRIES + 1e-06)
    factor = jnp.minimum(1.0, 1.0 / root_mean)

    def own_result():
        for expert in range(EXPERTS):
            new_ref[expert] = fresh(pair[expert, 0], pair[expert, 1], factor)

    def gram_copies():
        partner = along_slab(chip * CORES + 1 - core)
        return [
            send(
                gram_own.at[index],
                gram_other.at[index],
                gram_send.at[index],
                gram_recv.at[index],
                partner,
            )
            for index in range(3)
        ]

    def back_copy(hops_x, hops_y):
        place = hops_x * SIDE + hops_y
        if (hops_x, hops_y) in BACK_RELAYED:
            slot = BACK_RELAYED.index((hops_x, hops_y))
            if slot < 2:
                by = ((x + 3 + 2 * (x % 2)) % SIDE, y)
            else:
                by = (x, (y + hops_y) % SIDE)
            return send(
                outgoing.at[place],
                back_relayed.at[slot],
                back_send.at[place],
                back_relay_recv.at[slot],
                along_slab(device_of(*by)),
            )
        target = device_of((x + hops_x) % SIDE, (y + hops_y) % SIDE)
        return send(
            outgoing.at[place],
            update_ref.at[mine],
            back_send.at[place],
            back_recv.at[mine],
            along_slab(target),
        )

    def back_forward(slot):
        hops_x, hops_y = BACK_RELAYED[slot]
        if slot < 2:
            of_x, of_y = (x + 3 + 2 * (x % 2)) % SIDE, y
        else:
            of_x, of_y = x, (y + SIDE - hops_y) % SIDE
        expert = of_x * 2 + of_y // 2
        return send(
            back_relayed.at[slot],
            update_ref.at[expert],
            back_relay_send.at[slot],
            back_recv.at[expert],
            along_slab(device_of((of_x + hops_x) % SIDE, (of_y + hops_y) % SIDE)),
        )

    def back_wait(slot):
        send(
            outgoing.at[0],
            back_relayed.at[slot],
            back_send.at[0],
            back_relay_recv.at[slot],
            along_slab(slab),
        ).wait_recv()

    @pl.when(active)
    def _():
        local_copy.wait()

        @pl.loop(1, CHIPS)
        def _(place):
            send(
                pair.at[0], raw.at[place], raw_send.at[0], raw_recv.at[place], along_slab(slab)
            ).wait_recv()

        for place in range(CHIPS):
            own_new[place * ROWS : (place + 1) * ROWS, :] = fresh(
                raw[place, 0], raw[place, 1], factor
            )

        for index, (left, right) in enumerate(((0, 0), (0, 1), (1, 1))):
            gram_own[index] = lax.dot_general(
                own_new[:, left * HALF : (left + 1) * HALF],
                own_new[:, right * HALF : (right + 1) * HALF],
                (((0,), (0,)), ((), ())),
                preferred_element_type=jnp.float32,
            )
            if index > 0:
                gram_copies()[index - 1].start()
        gram_copies()[2].start()
        for copy in gram_copies():
            copy.wait_recv()

        trace = jnp.zeros((128, 128), jnp.float32)
        for index in (0, 2):
            whole = gram_own[index] + gram_other[index]
            gram_own_low, gram_own_high = whole[:128, :128], whole[128:, 128:]
            trace += gram_own_low + gram_own_high
        eye = lax.broadcasted_iota(jnp.int32, (128, 128), 0) == lax.broadcasted_iota(
            jnp.int32, (128, 128), 1
        )
        trace = jnp.where(eye, trace, 0.0)
        frobenius = (
            jnp.sum(jnp.sum(trace, axis=0, keepdims=True), axis=1, keepdims=True) + 1e-06
        )
        inverse = 1.0 / frobenius
        for index, (left, right) in enumerate(((0, 0), (0, 1), (1, 1))):
            block = (gram_own[index] + gram_other[index]) * inverse
            current[left * HALF : (left + 1) * HALF, right * HALF : (right + 1) * HALF] = block
            rounded[left * HALF : (left + 1) * HALF, right * HALF : (right + 1) * HALF] = (
                block.astype(jnp.bfloat16)
            )
            if index == 1:
                block = block.T
                current[HALF:, :HALF] = block
                rounded[HALF:, :HALF] = block.astype(jnp.bfloat16)

        def polynomial(into, start):
            rows = slice(start, start + HALF)
            squared = dot(rounded[rows, :], rounded[...])
            diagonal = lax.broadcasted_iota(jnp.int32, (HALF, K), 0) + start
            identity = jnp.where(
                diagonal == lax.broadcasted_iota(jnp.int32, (HALF, K), 1), COEF_A, 0.0
            )
            into[rows, :] = (identity + COEF_B * current[rows, :] + COEF_C * squared).astype(
                jnp.bfloat16
            )

        halves = (0, HALF)
        for start in halves:
            polynomial(poly_first, start)
        for start in halves:
            rows = slice(start, start + HALF)
            halfway[rows, :] = dot(rounded[rows, :], poly_first[...]).astype(jnp.bfloat16)
        for start in halves:
            rows = slice(start, start + HALF)
            following = dot(poly_first[rows, :], halfway[...])
            current[rows, :] = following
            rounded[rows, :] = following.astype(jnp.bfloat16)
        for start in halves:
            polynomial(poly_second, start)
        root = 1.0 / jnp.sqrt(frobenius)
        for start in halves:
            rows = slice(start, start + HALF)
            scaled[rows, :] = (dot(poly_first[rows, :], poly_second[...]) * root).astype(
                jnp.bfloat16
            )

        for turn, hops_x in enumerate(COLUMNS):
            start = hops_x * SIDE * ROWS
            result = jnp.sqrt(jnp.float32(M)) * dot(
                own_new[start : start + SIDE * ROWS, :], scaled[...]
            )
            outgoing[hops_x * SIDE : (hops_x + 1) * SIDE] = result.astype(jnp.bfloat16).reshape(
                SIDE, ROWS, K
            )
            if turn > 0:
                for hops_y in COLUMNS:
                    back_copy(COLUMNS[turn - 1], hops_y).start()
        for hops_y in COLUMNS[:-1]:
            back_copy(0, hops_y).start()
        update_ref[mine] = outgoing[0]

    own_result()

    @pl.when(jnp.logical_not(active))
    def _():
        for slot in range(len(BACK_RELAYED)):
            back_wait(slot)
            back_forward(slot).start()

    for hops in COLUMNS:
        for which in range(2):
            expert, column, row, from_x, from_y, index = raw_route(hops, which)

            @pl.when(device_of(column, row) != slab)
            def _():
                raw_direct(hops, which).wait_send()
                send(
                    outgoing.at[0],
                    update_ref.at[expert],
                    back_send.at[0],
                    back_recv.at[expert],
                    along_slab(slab),
                ).wait_recv()

    @pl.when(jnp.logical_not(active))
    def _():
        for slot in range(len(BACK_RELAYED)):
            relay_forward(slot).wait_send()
            back_forward(slot).wait_send()

    @pl.when(active)
    def _():
        for copy in gram_copies():
            copy.wait_send()
        for hops_x in COLUMNS:
            for hops_y in COLUMNS:
                if (hops_x, hops_y) != (0, 0):
                    back_copy(hops_x, hops_y).wait_send()

    @pl.loop(1, SLABS)
    def _(step):
        slab_copy(step).wait_send()

    for copy in near_copies + window_copies + far_copies:
        copy.wait_send()


def on_device(grads, grad_slot, momentum):
    shape = jax.ShapeDtypeStruct(grads.shape, jnp.bfloat16)
    scalar = (1, 128)
    dma = pltpu.SemaphoreType.DMA
    return pl.pallas_call(
        kernel,
        out_shape=(shape, shape),
        in_specs=[
            pl.BlockSpec(memory_space=pltpu.HBM),
            pl.BlockSpec(memory_space=pltpu.HBM),
            pl.BlockSpec(memory_space=pltpu.HBM),
        ],
        out_specs=(pl.BlockSpec(memory_space=pltpu.VMEM),) * 2,
        scratch_shapes=[
            pltpu.SMEM((1, EXPERTS), jnp.int32),
            pltpu.VMEM((EXPERTS, ROWS, K), jnp.bfloat16),
            pltpu.VMEM((EXPERTS, 2, ROWS, K), jnp.bfloat16),
            pltpu.VMEM((CHIPS, 2, ROWS, K), jnp.bfloat16),
            pltpu.VMEM((len(BACK_RELAYED), 2, ROWS, K), jnp.bfloat16),
            pltpu.VMEM((len(BACK_RELAYED), ROWS, K), jnp.bfloat16),
            pltpu.VMEM((OWN, K), jnp.bfloat16),
            pltpu.VMEM(scalar, jnp.float32),
            pltpu.VMEM((SLABS, *scalar), jnp.float32),
            pltpu.VMEM(scalar, jnp.float32),
            pltpu.VMEM((len(NEAR), *scalar), jnp.float32),
            pltpu.VMEM(scalar, jnp.float32),
            pltpu.VMEM((2, *scalar), jnp.float32),
            pltpu.VMEM(scalar, jnp.float32),
            pltpu.VMEM((2, *scalar), jnp.float32),
            pltpu.VMEM((3, HALF, HALF), jnp.float32),
            pltpu.VMEM((3, HALF, HALF), jnp.float32),
            pltpu.VMEM((K, K), jnp.float32),
            pltpu.VMEM((K, K), jnp.bfloat16),
            pltpu.VMEM((K, K), jnp.bfloat16),
            pltpu.VMEM((K, K), jnp.bfloat16),
            pltpu.VMEM((K, K), jnp.bfloat16),
            pltpu.VMEM((K, K), jnp.bfloat16),
            pltpu.VMEM((CHIPS, ROWS, K), jnp.bfloat16),
            dma((3,)),
            dma((SLABS,)),
            dma((SLABS,)),
            dma((len(NEAR),)),
            dma((len(NEAR),)),
            dma((2, 2)),
            dma((2, 2)),
            dma((EXPERTS,)),
            dma((CHIPS,)),
            dma((len(BACK_RELAYED),)),
            dma((len(BACK_RELAYED),)),
            dma((1,)),
            dma((3,)),
            dma((3,)),
            dma((CHIPS,)),
            dma((EXPERTS,)),
            dma((len(BACK_RELAYED),)),
            dma((len(BACK_RELAYED),)),
        ],
        compiler_params=pltpu.CompilerParams(
            collective_id=0, has_side_effects=True, vmem_limit_bytes=48 * 1024 * 1024
        ),
        name="muon_step",
    )(grad_slot, grads, momentum)


def solution(mesh):
    in_specs = (P("group", "slab", None), P("group", None), P("group", "slab", None))
    out_specs = (P("group", "slab", None), P("group", "slab", None))
    return jax.shard_map(
        on_device, mesh=mesh, in_specs=in_specs, out_specs=out_specs, check_vma=False
    )
```

```python
import jax
import jax.numpy as jnp
from jax import lax
from jax.experimental import pallas as pl
from jax.experimental.pallas import tpu as pltpu
from jax.sharding import PartitionSpec as P

MESH = pl.DeviceIdType.MESH

SIDE = 4
CORES = 2
SLABS = SIDE * SIDE * CORES
CHIPS = SIDE * SIDE
GROUPS = 32
EXPERTS = 8
ROWS = 64
M = SLABS * ROWS
K = 512
HALF = K // 2
OWN = CHIPS * ROWS
REACH = 4

COEF_A = 3.4445
COEF_B = -4.775
COEF_C = 2.0315
DECAY_RATE = 0.95
ENTRIES = GROUPS * EXPERTS * M * K

COLUMNS = (2, 1, 3, 0)
BACK_RELAYED = ((2, 1), (2, 3), (1, 1), (3, 3))
NEAR = tuple(off for off in range(-REACH, REACH) if off != 0)


def squares(block):
    wide = block.astype(jnp.float32)
    return jnp.sum((wide * wide).reshape(ROWS // 8, 8, K), axis=0)


def fresh(moment, gradient, factor):
    return (
        DECAY_RATE * moment.astype(jnp.float32) + factor * gradient.astype(jnp.float32)
    ).astype(jnp.bfloat16)


def dot(left, right):
    return jnp.dot(left, right, preferred_element_type=jnp.float32)


def kernel(
    slot_hbm,
    grads_hbm,
    momentum_hbm,
    new_ref,
    update_ref,
    slot_ref,
    grads_in,
    pair,
    raw,
    relayed,
    back_relayed,
    fresh_out,
    own_new,
    part,
    slab_parts,
    plane,
    near_parts,
    window,
    window_parts,
    wide_window,
    far_parts,
    gram_own,
    gram_other,
    current,
    rounded,
    poly_first,
    halfway,
    poly_second,
    scaled,
    outgoing,
    load_sem,
    slab_send,
    slab_recv,
    near_send,
    near_recv,
    step_send,
    step_recv,
    raw_send,
    raw_recv,
    relay_send,
    relay_recv,
    local_sem,
    gram_send,
    gram_recv,
    back_send,
    back_recv,
    back_relay_send,
    back_relay_recv,
):
    slab = lax.axis_index("slab")
    group = lax.axis_index("group")
    chip = slab // CORES
    core = slab % CORES
    x = chip // SIDE
    y = chip % SIDE
    active = (x + y) % 2 == 0
    mine = x * 2 + y // 2

    def along_slab(other):
        return (other, group)

    def device_of(at_x, at_y):
        return (at_x * SIDE + at_y) * CORES + core

    def along_group(offset):
        return (slab, (group + offset + GROUPS) % GROUPS)

    def send(src, dst, send_sem, recv_sem, device):
        return pltpu.make_async_remote_copy(
            src_ref=src,
            dst_ref=dst,
            send_sem=send_sem,
            recv_sem=recv_sem,
            device_id=device,
            device_id_type=MESH,
        )

    load_grads = pltpu.make_async_copy(grads_hbm, grads_in, load_sem.at[0])
    load_momentum = pltpu.make_async_copy(momentum_hbm, pair.at[:, 0], load_sem.at[1])
    load_slots = pltpu.make_async_copy(slot_hbm, slot_ref, load_sem.at[2])
    load_slots.start()
    load_grads.start()
    load_momentum.start()

    barrier = pltpu.get_barrier_semaphore()
    for offset in NEAR + (REACH,):
        pl.semaphore_signal(barrier, inc=1, device_id=along_group(offset), device_id_type=MESH)

    @pl.loop(1, SLABS)
    def _(step):
        pl.semaphore_signal(
            barrier, inc=1, device_id=along_slab((slab + step) % SLABS), device_id_type=MESH
        )

    load_slots.wait()
    load_grads.wait()
    total = jnp.zeros((8, K), jnp.float32)
    for expert in range(EXPERTS):
        block = grads_in[slot_ref[0, expert]]
        pair[expert, 1] = block
        total += squares(block)
    lanes = total[:, :128] + total[:, 128:256] + total[:, 256:384] + total[:, 384:]
    part[...] = jnp.sum(lanes, axis=0, keepdims=True)
    load_momentum.wait()
    pl.semaphore_wait(barrier, SLABS - 1 + len(NEAR) + 1)

    def slab_copy(step):
        return send(
            part,
            slab_parts.at[step],
            slab_send.at[step],
            slab_recv.at[step],
            along_slab((slab + step) % SLABS),
        )

    @pl.loop(1, SLABS)
    def _(step):
        slab_copy(step).start()

    def raw_route(hops, which):
        column = (x + hops) % SIDE
        row = which * 2 + column % 2
        return (
            column * 2 + which,
            column,
            row,
            (SIDE - hops) % SIDE,
            (y + SIDE - row) % SIDE,
            COLUMNS.index(hops) * 2 + which,
        )

    def raw_direct(hops, which):
        expert, column, row, from_x, from_y, index = raw_route(hops, which)
        place = from_x * SIDE + from_y
        return send(
            pair.at[expert],
            raw.at[place],
            raw_send.at[index],
            raw_recv.at[place],
            along_slab(device_of(column, row)),
        )

    def raw_relayed(hops, which, slot, by_x, by_y):
        expert, column, row, from_x, from_y, index = raw_route(hops, which)
        return send(
            pair.at[expert],
            relayed.at[slot],
            raw_send.at[index],
            relay_recv.at[slot],
            along_slab(device_of((column + by_x) % SIDE, (row + by_y) % SIDE)),
        )

    def relay_forward(slot):
        if slot < 2:
            towards = (x, (y + 1 + 2 * (y % 2)) % SIDE)
            place = (1 + 2 * slot) * SIDE + 2
        else:
            towards = ((x + (3 if slot == 2 else 1)) % SIDE, y)
            place = 5 if slot == 2 else 15
        return send(
            relayed.at[slot],
            raw.at[place],
            relay_send.at[slot],
            raw_recv.at[place],
            along_slab(device_of(*towards)),
        )

    def relay_wait(slot):
        send(
            pair.at[0], relayed.at[slot], raw_send.at[0], relay_recv.at[slot], along_slab(slab)
        ).wait_recv()

    def relay(slots):
        @pl.when(jnp.logical_not(active))
        def _():
            for slot in slots:
                relay_wait(slot)
                relay_forward(slot).start()

    local_copy = pltpu.make_async_copy(pair.at[mine], raw.at[0], local_sem.at[0])

    @pl.loop(1, SLABS)
    def _(step):
        slab_copy(step).wait_recv()

    plane[...] = part[...] + jnp.sum(slab_parts[1:], axis=0)

    near_copies = [
        send(
            plane,
            near_parts.at[index],
            near_send.at[index],
            near_recv.at[index],
            along_group(offset),
        )
        for index, offset in enumerate(NEAR)
    ]

    def step_copies(src, dst, stage, reach):
        return [
            send(
                src,
                dst.at[side],
                step_send.at[stage, side],
                step_recv.at[stage, side],
                along_group(offset),
            )
            for side, offset in enumerate((reach, -reach))
        ]

    window_copies = step_copies(window, window_parts, 0, REACH)
    far_copies = step_copies(wide_window, far_parts, 1, 2 * REACH)

    for copy in near_copies:
        copy.start()

    for hops, diagonal in ((1, 3), (3, 1)):
        for which in range(2):
            from_y = raw_route(hops, which)[4]
            row = raw_route(hops, which)[2]

            @pl.when(from_y == diagonal)
            def _():
                raw_relayed(hops, which, 2 if diagonal == 1 else 3, SIDE - hops, 0).start()

            @pl.when(from_y == 2)
            def _():
                raw_relayed(
                    hops, which, 1 if diagonal == 3 else 0, 0, 1 + 2 * (row % 2)
                ).start()

    for hops in COLUMNS:
        for which in range(2):
            from_y = raw_route(hops, which)[4]
            if hops == 0:
                direct = from_y != 0
            elif hops == 2:
                direct = True
            else:
                direct = jnp.logical_and(from_y != 2, from_y != SIDE - hops)

            @pl.when(direct)
            def _():
                raw_direct(hops, which).start()

    @pl.when(active)
    def _():
        local_copy.start()

    for copy in near_copies:
        copy.wait_recv()
    window[...] = plane[...] + jnp.sum(near_parts[...], axis=0)
    for copy in window_copies:
        copy.start()
    for copy in window_copies:
        copy.wait_recv()
    wide_window[...] = jnp.sum(window_parts[...], axis=0)
    for copy in far_copies:
        copy.start()
    relay((2, 3, 0, 1))
    for copy in far_copies:
        copy.wait_recv()

    total_sq = jnp.sum(jnp.sum(far_parts[...], axis=0), axis=1, keepdims=True)
    root_mean = jnp.sqrt(total_sq / ENTRIES + 1e-06)
    factor = jnp.minimum(1.0, 1.0 / root_mean)

    def own_result():
        for expert in range(EXPERTS):
            fresh_out[expert] = fresh(pair[expert, 0], pair[expert, 1], factor)

    def gram_copies():
        partner = along_slab(chip * CORES + 1 - core)
        return [
            send(
                gram_own.at[index],
                gram_other.at[index],
                gram_send.at[index],
                gram_recv.at[index],
                partner,
            )
            for index in range(3)
        ]

    def back_copy(hops_x, hops_y):
        place = hops_x * SIDE + hops_y
        if (hops_x, hops_y) in BACK_RELAYED:
            slot = BACK_RELAYED.index((hops_x, hops_y))
            if slot < 2:
                by = ((x + 3 + 2 * (x % 2)) % SIDE, y)
            else:
                by = (x, (y + hops_y) % SIDE)
            return send(
                outgoing.at[place],
                back_relayed.at[slot],
                back_send.at[place],
                back_relay_recv.at[slot],
                along_slab(device_of(*by)),
            )
        target = device_of((x + hops_x) % SIDE, (y + hops_y) % SIDE)
        return send(
            outgoing.at[place],
            update_ref.at[mine],
            back_send.at[place],
            back_recv.at[mine],
            along_slab(target),
        )

    def back_forward(slot):
        hops_x, hops_y = BACK_RELAYED[slot]
        if slot < 2:
            of_x, of_y = (x + 3 + 2 * (x % 2)) % SIDE, y
        else:
            of_x, of_y = x, (y + SIDE - hops_y) % SIDE
        expert = of_x * 2 + of_y // 2
        return send(
            back_relayed.at[slot],
            update_ref.at[expert],
            back_relay_send.at[slot],
            back_recv.at[expert],
            along_slab(device_of((of_x + hops_x) % SIDE, (of_y + hops_y) % SIDE)),
        )

    def back_wait(slot):
        send(
            outgoing.at[0],
            back_relayed.at[slot],
            back_send.at[0],
            back_relay_recv.at[slot],
            along_slab(slab),
        ).wait_recv()

    @pl.when(active)
    def _():
        local_copy.wait()

        for place in range(CHIPS):
            if place > 0:
                send(
                    pair.at[0], raw.at[place], raw_send.at[0], raw_recv.at[place], along_slab(slab)
                ).wait_recv()
            own_new[place * ROWS : (place + 1) * ROWS, :] = fresh(
                raw[place, 0], raw[place, 1], factor
            )

        for index, (left, right) in enumerate(((0, 0), (0, 1), (1, 1))):
            gram_own[index] = lax.dot_general(
                own_new[:, left * HALF : (left + 1) * HALF],
                own_new[:, right * HALF : (right + 1) * HALF],
                (((0,), (0,)), ((), ())),
                preferred_element_type=jnp.float32,
            )
            if index > 0:
                gram_copies()[index - 1].start()
        gram_copies()[2].start()
        for copy in gram_copies():
            copy.wait_recv()

        trace = jnp.zeros((128, 128), jnp.float32)
        for index in (0, 2):
            whole = gram_own[index] + gram_other[index]
            gram_own_low, gram_own_high = whole[:128, :128], whole[128:, 128:]
            trace += gram_own_low + gram_own_high
        eye = lax.broadcasted_iota(jnp.int32, (128, 128), 0) == lax.broadcasted_iota(
            jnp.int32, (128, 128), 1
        )
        trace = jnp.where(eye, trace, 0.0)
        frobenius = (
            jnp.sum(jnp.sum(trace, axis=0, keepdims=True), axis=1, keepdims=True) + 1e-06
        )
        inverse = 1.0 / frobenius
        for index, (left, right) in enumerate(((0, 0), (0, 1), (1, 1))):
            block = (gram_own[index] + gram_other[index]) * inverse
            current[left * HALF : (left + 1) * HALF, right * HALF : (right + 1) * HALF] = block
            rounded[left * HALF : (left + 1) * HALF, right * HALF : (right + 1) * HALF] = (
                block.astype(jnp.bfloat16)
            )
            if index == 1:
                block = block.T
                current[HALF:, :HALF] = block
                rounded[HALF:, :HALF] = block.astype(jnp.bfloat16)

        def polynomial(into, start):
            rows = slice(start, start + HALF)
            squared = dot(rounded[rows, :], rounded[...])
            diagonal = lax.broadcasted_iota(jnp.int32, (HALF, K), 0) + start
            identity = jnp.where(
                diagonal == lax.broadcasted_iota(jnp.int32, (HALF, K), 1), COEF_A, 0.0
            )
            into[rows, :] = (identity + COEF_B * current[rows, :] + COEF_C * squared).astype(
                jnp.bfloat16
            )

        halves = (0, HALF)
        for start in halves:
            polynomial(poly_first, start)
        for start in halves:
            rows = slice(start, start + HALF)
            halfway[rows, :] = dot(rounded[rows, :], poly_first[...]).astype(jnp.bfloat16)
        for start in halves:
            rows = slice(start, start + HALF)
            following = dot(poly_first[rows, :], halfway[...])
            current[rows, :] = following
            rounded[rows, :] = following.astype(jnp.bfloat16)
        for start in halves:
            polynomial(poly_second, start)
        root = 1.0 / jnp.sqrt(frobenius)
        for start in halves:
            rows = slice(start, start + HALF)
            scaled[rows, :] = (dot(poly_first[rows, :], poly_second[...]) * root).astype(
                jnp.bfloat16
            )

        for turn, hops_x in enumerate(COLUMNS):
            start = hops_x * SIDE * ROWS
            result = jnp.sqrt(jnp.float32(M)) * dot(
                own_new[start : start + SIDE * ROWS, :], scaled[...]
            )
            outgoing[hops_x * SIDE : (hops_x + 1) * SIDE] = result.astype(jnp.bfloat16).reshape(
                SIDE, ROWS, K
            )
            if turn > 0:
                for hops_y in COLUMNS:
                    back_copy(COLUMNS[turn - 1], hops_y).start()
        for hops_y in COLUMNS[:-1]:
            back_copy(0, hops_y).start()
        pltpu.make_async_copy(outgoing.at[0], update_ref.at[mine], local_sem.at[1]).start()

    own_result()
    new_copy = pltpu.make_async_copy(fresh_out, new_ref, load_sem.at[3])
    new_copy.start()

    @pl.when(jnp.logical_not(active))
    def _():
        for slot in range(len(BACK_RELAYED)):
            back_wait(slot)
            back_forward(slot).start()

    for hops in COLUMNS:
        for which in range(2):
            expert, column, row, from_x, from_y, index = raw_route(hops, which)

            @pl.when(device_of(column, row) != slab)
            def _():
                raw_direct(hops, which).wait_send()
                send(
                    outgoing.at[0],
                    update_ref.at[expert],
                    back_send.at[0],
                    back_recv.at[expert],
                    along_slab(slab),
                ).wait_recv()

    @pl.when(jnp.logical_not(active))
    def _():
        for slot in range(len(BACK_RELAYED)):
            relay_forward(slot).wait_send()
            back_forward(slot).wait_send()

    new_copy.wait()

    @pl.when(active)
    def _():
        pltpu.make_async_copy(outgoing.at[0], update_ref.at[mine], local_sem.at[1]).wait()
        for copy in gram_copies():
            copy.wait_send()
        for hops_x in COLUMNS:
            for hops_y in COLUMNS:
                if (hops_x, hops_y) != (0, 0):
                    back_copy(hops_x, hops_y).wait_send()

    @pl.loop(1, SLABS)
    def _(step):
        slab_copy(step).wait_send()

    for copy in near_copies + window_copies + far_copies:
        copy.wait_send()


def finish_kernel(new_ref, update_ref, new_out, update_out, sem):
    copies = (
        pltpu.make_async_copy(new_ref, new_out, sem.at[0]),
        pltpu.make_async_copy(update_ref, update_out, sem.at[1]),
    )
    for copy in copies:
        copy.start()
    for copy in copies:
        copy.wait()


def finish(new, update):
    anywhere = (pl.BlockSpec(memory_space=pl.ANY),) * 2
    return pl.pallas_call(
        finish_kernel,
        out_shape=tuple(jax.ShapeDtypeStruct(a.shape, a.dtype) for a in (new, update)),
        in_specs=anywhere,
        out_specs=anywhere,
        scratch_shapes=[pltpu.SemaphoreType.DMA((2,))],
        compiler_params=pltpu.CompilerParams(vmem_limit_bytes=1024 * 1024),
        name="finish",
    )(new, update)


def on_device(grads, grad_slot, momentum):
    shape = pltpu.VMEM(grads.shape, jnp.bfloat16)
    grads, grad_slot, momentum = (
        pltpu.with_memory_space_constraint(a, pltpu.HBM) for a in (grads, grad_slot, momentum)
    )
    scalar = (1, 128)
    dma = pltpu.SemaphoreType.DMA
    return finish(*pl.pallas_call(
        kernel,
        out_shape=(shape, shape),
        in_specs=[
            pl.BlockSpec(memory_space=pltpu.HBM),
            pl.BlockSpec(memory_space=pltpu.HBM),
            pl.BlockSpec(memory_space=pltpu.HBM),
        ],
        out_specs=(pl.BlockSpec(memory_space=pl.ANY),) * 2,
        scratch_shapes=[
            pltpu.SMEM((1, EXPERTS), jnp.int32),
            pltpu.VMEM((EXPERTS, ROWS, K), jnp.bfloat16),
            pltpu.VMEM((EXPERTS, 2, ROWS, K), jnp.bfloat16),
            pltpu.VMEM((CHIPS, 2, ROWS, K), jnp.bfloat16),
            pltpu.VMEM((len(BACK_RELAYED), 2, ROWS, K), jnp.bfloat16),
            pltpu.VMEM((len(BACK_RELAYED), ROWS, K), jnp.bfloat16),
            pltpu.VMEM((EXPERTS, ROWS, K), jnp.bfloat16),
            pltpu.VMEM((OWN, K), jnp.bfloat16),
            pltpu.VMEM(scalar, jnp.float32),
            pltpu.VMEM((SLABS, *scalar), jnp.float32),
            pltpu.VMEM(scalar, jnp.float32),
            pltpu.VMEM((len(NEAR), *scalar), jnp.float32),
            pltpu.VMEM(scalar, jnp.float32),
            pltpu.VMEM((2, *scalar), jnp.float32),
            pltpu.VMEM(scalar, jnp.float32),
            pltpu.VMEM((2, *scalar), jnp.float32),
            pltpu.VMEM((3, HALF, HALF), jnp.float32),
            pltpu.VMEM((3, HALF, HALF), jnp.float32),
            pltpu.VMEM((K, K), jnp.float32),
            pltpu.VMEM((K, K), jnp.bfloat16),
            pltpu.VMEM((K, K), jnp.bfloat16),
            pltpu.VMEM((K, K), jnp.bfloat16),
            pltpu.VMEM((K, K), jnp.bfloat16),
            pltpu.VMEM((K, K), jnp.bfloat16),
            pltpu.VMEM((CHIPS, ROWS, K), jnp.bfloat16),
            dma((4,)),
            dma((SLABS,)),
            dma((SLABS,)),
            dma((len(NEAR),)),
            dma((len(NEAR),)),
            dma((2, 2)),
            dma((2, 2)),
            dma((EXPERTS,)),
            dma((CHIPS,)),
            dma((len(BACK_RELAYED),)),
            dma((len(BACK_RELAYED),)),
            dma((2,)),
            dma((3,)),
            dma((3,)),
            dma((CHIPS,)),
            dma((EXPERTS,)),
            dma((len(BACK_RELAYED),)),
            dma((len(BACK_RELAYED),)),
        ],
        compiler_params=pltpu.CompilerParams(
            collective_id=0, has_side_effects=True, vmem_limit_bytes=48 * 1024 * 1024
        ),
        name="muon_step",
    )(grad_slot, grads, momentum))


def solution(mesh):
    in_specs = (P("group", "slab", None), P("group", None), P("group", "slab", None))
    out_specs = (P("group", "slab", None), P("group", "slab", None))
    return jax.shard_map(
        on_device, mesh=mesh, in_specs=in_specs, out_specs=out_specs, check_vma=False
    )
```

```python
import jax
import jax.numpy as jnp
from jax import lax
from jax.experimental import pallas as pl
from jax.experimental.pallas import tpu as pltpu
from jax.sharding import PartitionSpec as P

MESH = pl.DeviceIdType.MESH

SIDE = 4
CORES = 2
SLABS = SIDE * SIDE * CORES
CHIPS = SIDE * SIDE
GROUPS = 32
EXPERTS = 8
ROWS = 64
M = SLABS * ROWS
K = 512
HALF = K // 2
OWN = CHIPS * ROWS
REACH = 4

COEF_A = 3.4445
COEF_B = -4.775
COEF_C = 2.0315
DECAY_RATE = 0.95
ENTRIES = GROUPS * EXPERTS * M * K

COLUMNS = (2, 1, 3, 0)
BACK_RELAYED = ((2, 1), (2, 3), (1, 1), (3, 3))
GREETED = tuple(off for off in range(-REACH, REACH + 1) if off != 0)
NEAR = tuple(sorted((off for off in range(-2 * REACH, 2 * REACH) if off != 0), key=lambda o: -abs(o)))


def squares(block):
    wide = block.astype(jnp.float32)
    return jnp.sum((wide * wide).reshape(ROWS // 8, 8, K), axis=0)


def fresh(moment, gradient, factor):
    return (
        DECAY_RATE * moment.astype(jnp.float32) + factor * gradient.astype(jnp.float32)
    ).astype(jnp.bfloat16)


def dot(left, right):
    return jnp.dot(left, right, preferred_element_type=jnp.float32)


def kernel(
    slot_hbm,
    grads_hbm,
    momentum_hbm,
    new_ref,
    update_ref,
    slot_ref,
    grads_in,
    pair,
    raw,
    relayed,
    back_relayed,
    fresh_out,
    own_new,
    part,
    slab_parts,
    plane,
    near_parts,
    window,
    far_parts,
    grand,
    gram_own,
    gram_other,
    current,
    rounded,
    poly_first,
    halfway,
    poly_second,
    scaled,
    outgoing,
    load_sem,
    slab_send,
    slab_recv,
    near_send,
    near_recv,
    far_send,
    far_recv,
    grand_send,
    grand_recv,
    greeting,
    passed,
    raw_send,
    raw_recv,
    relay_send,
    relay_recv,
    local_sem,
    gram_send,
    gram_recv,
    back_send,
    back_recv,
    back_relay_send,
    back_relay_recv,
):
    slab = lax.axis_index("slab")
    group = lax.axis_index("group")
    chip = slab // CORES
    core = slab % CORES
    x = chip // SIDE
    y = chip % SIDE
    active = (x + y) % 2 == 0
    mine = x * 2 + y // 2

    def along_slab(other):
        return (other, group)

    def device_of(at_x, at_y):
        return (at_x * SIDE + at_y) * CORES + core

    def along_group(offset):
        return (slab, (group + offset + GROUPS) % GROUPS)

    def send(src, dst, send_sem, recv_sem, device):
        return pltpu.make_async_remote_copy(
            src_ref=src,
            dst_ref=dst,
            send_sem=send_sem,
            recv_sem=recv_sem,
            device_id=device,
            device_id_type=MESH,
        )

    load_grads = pltpu.make_async_copy(grads_hbm, grads_in, load_sem.at[0])
    load_momentum = pltpu.make_async_copy(momentum_hbm, pair.at[:, 0], load_sem.at[1])
    load_slots = pltpu.make_async_copy(slot_hbm, slot_ref, load_sem.at[2])
    load_slots.start()
    load_grads.start()
    load_momentum.start()

    along = core == 1
    unseen = jnp.maximum(REACH - group, 0)
    barrier = pltpu.get_barrier_semaphore()

    @pl.when(along)
    def _():
        for offset in GREETED:

            @pl.when(group + offset < GROUPS)
            def _():
                pl.semaphore_signal(
                    barrier, inc=1, device_id=along_group(offset), device_id_type=MESH
                )

    @pl.loop(1, SLABS)
    def _(step):
        pl.semaphore_signal(
            barrier, inc=1, device_id=along_slab((slab + step) % SLABS), device_id_type=MESH
        )

    load_slots.wait()
    load_grads.wait()
    total = jnp.zeros((8, K), jnp.float32)
    for expert in range(EXPERTS):
        block = grads_in[slot_ref[0, expert]]
        pair[expert, 1] = block
        total += squares(block)
    lanes = total[:, :128] + total[:, 128:256] + total[:, 256:384] + total[:, 384:]
    part[...] = jnp.sum(lanes, axis=0, keepdims=True)
    load_momentum.wait()
    pl.semaphore_wait(barrier, SLABS - 1 + core * (len(GREETED) - unseen))

    def slab_copy(step):
        return send(
            part,
            slab_parts.at[step],
            slab_send.at[step],
            slab_recv.at[step],
            along_slab((slab + step) % SLABS),
        )

    @pl.loop(1, SLABS)
    def _(step):
        slab_copy(step).start()

    def pass_on():
        for side, offset in enumerate((REACH, -REACH)):
            pl.semaphore_signal(
                passed.at[side], inc=1, device_id=along_group(offset), device_id_type=MESH
            )

    @pl.when(along)
    def _():
        for offset in range(1, REACH + 1):

            @pl.when(group + offset >= GROUPS)
            def _():
                pl.semaphore_signal(
                    greeting, inc=1, device_id=along_group(offset), device_id_type=MESH
                )

        @pl.when(unseen == 0)
        def _():
            pass_on()

    def raw_route(hops, which):
        column = (x + hops) % SIDE
        row = which * 2 + column % 2
        return (
            column * 2 + which,
            column,
            row,
            (SIDE - hops) % SIDE,
            (y + SIDE - row) % SIDE,
            COLUMNS.index(hops) * 2 + which,
        )

    def raw_direct(hops, which):
        expert, column, row, from_x, from_y, index = raw_route(hops, which)
        place = from_x * SIDE + from_y
        return send(
            pair.at[expert],
            raw.at[place],
            raw_send.at[index],
            raw_recv.at[place],
            along_slab(device_of(column, row)),
        )

    def raw_relayed(hops, which, slot, by_x, by_y):
        expert, column, row, from_x, from_y, index = raw_route(hops, which)
        return send(
            pair.at[expert],
            relayed.at[slot],
            raw_send.at[index],
            relay_recv.at[slot],
            along_slab(device_of((column + by_x) % SIDE, (row + by_y) % SIDE)),
        )

    def relay_forward(slot):
        if slot < 2:
            towards = (x, (y + 1 + 2 * (y % 2)) % SIDE)
            place = (1 + 2 * slot) * SIDE + 2
        else:
            towards = ((x + (3 if slot == 2 else 1)) % SIDE, y)
            place = 5 if slot == 2 else 15
        return send(
            relayed.at[slot],
            raw.at[place],
            relay_send.at[slot],
            raw_recv.at[place],
            along_slab(device_of(*towards)),
        )

    def relay_wait(slot):
        send(
            pair.at[0], relayed.at[slot], raw_send.at[0], relay_recv.at[slot], along_slab(slab)
        ).wait_recv()

    def relay(slots):
        @pl.when(jnp.logical_not(active))
        def _():
            for slot in slots:
                relay_wait(slot)
                relay_forward(slot).start()

    local_copy = pltpu.make_async_copy(pair.at[mine], raw.at[0], local_sem.at[0])

    @pl.loop(1, SLABS)
    def _(step):
        slab_copy(step).wait_recv()

    plane[...] = part[...] + jnp.sum(slab_parts[1:], axis=0)

    near_copies = [
        send(
            plane,
            near_parts.at[index],
            near_send.at[index],
            near_recv.at[index],
            along_group(offset),
        )
        for index, offset in enumerate(NEAR)
    ]

    far_copies = [
        send(
            window,
            far_parts.at[side],
            far_send.at[side],
            far_recv.at[side],
            along_group(offset),
        )
        for side, offset in enumerate((2 * REACH, -2 * REACH))
    ]
    grand_copy = send(
        grand, grand, grand_send.at[0], grand_recv.at[0], along_slab(chip * CORES + 1 - core)
    )

    def start_near():
        for side in range(2):
            pl.semaphore_wait(passed.at[side], 1)
        for copy in near_copies:
            copy.start()

    @pl.when(jnp.logical_and(along, unseen == 0))
    def _():
        start_near()

    for hops, diagonal in ((1, 3), (3, 1)):
        for which in range(2):
            from_y = raw_route(hops, which)[4]
            row = raw_route(hops, which)[2]

            @pl.when(from_y == diagonal)
            def _():
                raw_relayed(hops, which, 2 if diagonal == 1 else 3, SIDE - hops, 0).start()

            @pl.when(from_y == 2)
            def _():
                raw_relayed(
                    hops, which, 1 if diagonal == 3 else 0, 0, 1 + 2 * (row % 2)
                ).start()

    for hops in COLUMNS:
        for which in range(2):
            from_y = raw_route(hops, which)[4]
            if hops == 0:
                direct = from_y != 0
            elif hops == 2:
                direct = True
            else:
                direct = jnp.logical_and(from_y != 2, from_y != SIDE - hops)

            @pl.when(direct)
            def _():
                raw_direct(hops, which).start()

    @pl.when(active)
    def _():
        local_copy.start()

    @pl.when(jnp.logical_and(along, unseen > 0))
    def _():
        pl.semaphore_wait(greeting, unseen)
        pass_on()
        start_near()

    @pl.when(along)
    def _():
        for copy in near_copies:
            copy.wait_recv()
        window[...] = plane[...] + jnp.sum(near_parts[...], axis=0)
        for copy in far_copies:
            copy.start()
        relay((2, 3, 0, 1))
        for copy in far_copies:
            copy.wait_recv()
        grand[...] = jnp.sum(far_parts[...], axis=0)
        grand_copy.start()

    @pl.when(jnp.logical_not(along))
    def _():
        relay((2, 3, 0, 1))
        grand_copy.wait_recv()

    total_sq = jnp.sum(grand[...], axis=1, keepdims=True)
    root_mean = jnp.sqrt(total_sq / ENTRIES + 1e-06)
    factor = jnp.minimum(1.0, 1.0 / root_mean)

    def own_result():
        for expert in range(EXPERTS):
            fresh_out[expert] = fresh(pair[expert, 0], pair[expert, 1], factor)

    def gram_copies():
        partner = along_slab(chip * CORES + 1 - core)
        return [
            send(
                gram_own.at[index],
                gram_other.at[index],
                gram_send.at[index],
                gram_recv.at[index],
                partner,
            )
            for index in range(3)
        ]

    def back_copy(hops_x, hops_y):
        place = hops_x * SIDE + hops_y
        if (hops_x, hops_y) in BACK_RELAYED:
            slot = BACK_RELAYED.index((hops_x, hops_y))
            if slot < 2:
                by = ((x + 3 + 2 * (x % 2)) % SIDE, y)
            else:
                by = (x, (y + hops_y) % SIDE)
            return send(
                outgoing.at[place],
                back_relayed.at[slot],
                back_send.at[place],
                back_relay_recv.at[slot],
                along_slab(device_of(*by)),
            )
        target = device_of((x + hops_x) % SIDE, (y + hops_y) % SIDE)
        return send(
            outgoing.at[place],
            update_ref.at[mine],
            back_send.at[place],
            back_recv.at[mine],
            along_slab(target),
        )

    def back_forward(slot):
        hops_x, hops_y = BACK_RELAYED[slot]
        if slot < 2:
            of_x, of_y = (x + 3 + 2 * (x % 2)) % SIDE, y
        else:
            of_x, of_y = x, (y + SIDE - hops_y) % SIDE
        expert = of_x * 2 + of_y // 2
        return send(
            back_relayed.at[slot],
            update_ref.at[expert],
            back_relay_send.at[slot],
            back_recv.at[expert],
            along_slab(device_of((of_x + hops_x) % SIDE, (of_y + hops_y) % SIDE)),
        )

    def back_wait(slot):
        send(
            outgoing.at[0],
            back_relayed.at[slot],
            back_send.at[0],
            back_relay_recv.at[slot],
            along_slab(slab),
        ).wait_recv()

    @pl.when(active)
    def _():
        local_copy.wait()

        for place in range(CHIPS):
            if place > 0:
                send(
                    pair.at[0], raw.at[place], raw_send.at[0], raw_recv.at[place], along_slab(slab)
                ).wait_recv()
            own_new[place * ROWS : (place + 1) * ROWS, :] = fresh(
                raw[place, 0], raw[place, 1], factor
            )

        for index, (left, right) in enumerate(((0, 0), (0, 1), (1, 1))):
            gram_own[index] = lax.dot_general(
                own_new[:, left * HALF : (left + 1) * HALF],
                own_new[:, right * HALF : (right + 1) * HALF],
                (((0,), (0,)), ((), ())),
                preferred_element_type=jnp.float32,
            )
            if index > 0:
                gram_copies()[index - 1].start()
        gram_copies()[2].start()
        for copy in gram_copies():
            copy.wait_recv()

        trace = jnp.zeros((128, 128), jnp.float32)
        for index in (0, 2):
            whole = gram_own[index] + gram_other[index]
            gram_own_low, gram_own_high = whole[:128, :128], whole[128:, 128:]
            trace += gram_own_low + gram_own_high
        eye = lax.broadcasted_iota(jnp.int32, (128, 128), 0) == lax.broadcasted_iota(
            jnp.int32, (128, 128), 1
        )
        trace = jnp.where(eye, trace, 0.0)
        frobenius = (
            jnp.sum(jnp.sum(trace, axis=0, keepdims=True), axis=1, keepdims=True) + 1e-06
        )
        inverse = 1.0 / frobenius
        for index, (left, right) in enumerate(((0, 0), (0, 1), (1, 1))):
            block = (gram_own[index] + gram_other[index]) * inverse
            current[left * HALF : (left + 1) * HALF, right * HALF : (right + 1) * HALF] = block
            rounded[left * HALF : (left + 1) * HALF, right * HALF : (right + 1) * HALF] = (
                block.astype(jnp.bfloat16)
            )
            if index == 1:
                block = block.T
                current[HALF:, :HALF] = block
                rounded[HALF:, :HALF] = block.astype(jnp.bfloat16)

        def polynomial(into, start):
            rows = slice(start, start + HALF)
            squared = dot(rounded[rows, :], rounded[...])
            diagonal = lax.broadcasted_iota(jnp.int32, (HALF, K), 0) + start
            identity = jnp.where(
                diagonal == lax.broadcasted_iota(jnp.int32, (HALF, K), 1), COEF_A, 0.0
            )
            into[rows, :] = (identity + COEF_B * current[rows, :] + COEF_C * squared).astype(
                jnp.bfloat16
            )

        halves = (0, HALF)
        for start in halves:
            polynomial(poly_first, start)
        for start in halves:
            rows = slice(start, start + HALF)
            halfway[rows, :] = dot(rounded[rows, :], poly_first[...]).astype(jnp.bfloat16)
        for start in halves:
            rows = slice(start, start + HALF)
            following = dot(poly_first[rows, :], halfway[...])
            current[rows, :] = following
            rounded[rows, :] = following.astype(jnp.bfloat16)
        for start in halves:
            polynomial(poly_second, start)
        root = 1.0 / jnp.sqrt(frobenius)
        for start in halves:
            rows = slice(start, start + HALF)
            scaled[rows, :] = (dot(poly_first[rows, :], poly_second[...]) * root).astype(
                jnp.bfloat16
            )

        for turn, hops_x in enumerate(COLUMNS):
            start = hops_x * SIDE * ROWS
            result = jnp.sqrt(jnp.float32(M)) * dot(
                own_new[start : start + SIDE * ROWS, :], scaled[...]
            )
            outgoing[hops_x * SIDE : (hops_x + 1) * SIDE] = result.astype(jnp.bfloat16).reshape(
                SIDE, ROWS, K
            )
            if turn > 0:
                for hops_y in COLUMNS:
                    back_copy(COLUMNS[turn - 1], hops_y).start()
        for hops_y in COLUMNS[:-1]:
            back_copy(0, hops_y).start()
        pltpu.make_async_copy(outgoing.at[0], update_ref.at[mine], local_sem.at[1]).start()

    own_result()
    new_copy = pltpu.make_async_copy(fresh_out, new_ref, load_sem.at[3])
    new_copy.start()

    @pl.when(jnp.logical_not(active))
    def _():
        for slot in range(len(BACK_RELAYED)):
            back_wait(slot)
            back_forward(slot).start()

    for hops in COLUMNS:
        for which in range(2):
            expert, column, row, from_x, from_y, index = raw_route(hops, which)

            @pl.when(device_of(column, row) != slab)
            def _():
                raw_direct(hops, which).wait_send()
                send(
                    outgoing.at[0],
                    update_ref.at[expert],
                    back_send.at[0],
                    back_recv.at[expert],
                    along_slab(slab),
                ).wait_recv()

    @pl.when(jnp.logical_not(active))
    def _():
        for slot in range(len(BACK_RELAYED)):
            relay_forward(slot).wait_send()
            back_forward(slot).wait_send()

    new_copy.wait()

    @pl.when(active)
    def _():
        pltpu.make_async_copy(outgoing.at[0], update_ref.at[mine], local_sem.at[1]).wait()
        for copy in gram_copies():
            copy.wait_send()
        for hops_x in COLUMNS:
            for hops_y in COLUMNS:
                if (hops_x, hops_y) != (0, 0):
                    back_copy(hops_x, hops_y).wait_send()

    @pl.loop(1, SLABS)
    def _(step):
        slab_copy(step).wait_send()

    @pl.when(along)
    def _():
        for copy in near_copies + far_copies + [grand_copy]:
            copy.wait_send()


def finish_kernel(new_ref, update_ref, new_out, update_out, sem):
    copies = (
        pltpu.make_async_copy(new_ref, new_out, sem.at[0]),
        pltpu.make_async_copy(update_ref, update_out, sem.at[1]),
    )
    for copy in copies:
        copy.start()
    for copy in copies:
        copy.wait()


def finish(new, update):
    anywhere = (pl.BlockSpec(memory_space=pl.ANY),) * 2
    return pl.pallas_call(
        finish_kernel,
        out_shape=tuple(jax.ShapeDtypeStruct(a.shape, a.dtype) for a in (new, update)),
        in_specs=anywhere,
        out_specs=anywhere,
        scratch_shapes=[pltpu.SemaphoreType.DMA((2,))],
        compiler_params=pltpu.CompilerParams(vmem_limit_bytes=1024 * 1024),
        name="finish",
    )(new, update)


def on_device(grads, grad_slot, momentum):
    shape = pltpu.VMEM(grads.shape, jnp.bfloat16)
    grads, grad_slot, momentum = (
        pltpu.with_memory_space_constraint(a, pltpu.HBM) for a in (grads, grad_slot, momentum)
    )
    scalar = (1, 128)
    dma = pltpu.SemaphoreType.DMA
    return finish(*pl.pallas_call(
        kernel,
        out_shape=(shape, shape),
        in_specs=[
            pl.BlockSpec(memory_space=pltpu.HBM),
            pl.BlockSpec(memory_space=pltpu.HBM),
            pl.BlockSpec(memory_space=pltpu.HBM),
        ],
        out_specs=(pl.BlockSpec(memory_space=pl.ANY),) * 2,
        scratch_shapes=[
            pltpu.SMEM((1, EXPERTS), jnp.int32),
            pltpu.VMEM((EXPERTS, ROWS, K), jnp.bfloat16),
            pltpu.VMEM((EXPERTS, 2, ROWS, K), jnp.bfloat16),
            pltpu.VMEM((CHIPS, 2, ROWS, K), jnp.bfloat16),
            pltpu.VMEM((len(BACK_RELAYED), 2, ROWS, K), jnp.bfloat16),
            pltpu.VMEM((len(BACK_RELAYED), ROWS, K), jnp.bfloat16),
            pltpu.VMEM((EXPERTS, ROWS, K), jnp.bfloat16),
            pltpu.VMEM((OWN, K), jnp.bfloat16),
            pltpu.VMEM(scalar, jnp.float32),
            pltpu.VMEM((SLABS, *scalar), jnp.float32),
            pltpu.VMEM(scalar, jnp.float32),
            pltpu.VMEM((len(NEAR), *scalar), jnp.float32),
            pltpu.VMEM(scalar, jnp.float32),
            pltpu.VMEM((2, *scalar), jnp.float32),
            pltpu.VMEM(scalar, jnp.float32),
            pltpu.VMEM((3, HALF, HALF), jnp.float32),
            pltpu.VMEM((3, HALF, HALF), jnp.float32),
            pltpu.VMEM((K, K), jnp.float32),
            pltpu.VMEM((K, K), jnp.bfloat16),
            pltpu.VMEM((K, K), jnp.bfloat16),
            pltpu.VMEM((K, K), jnp.bfloat16),
            pltpu.VMEM((K, K), jnp.bfloat16),
            pltpu.VMEM((K, K), jnp.bfloat16),
            pltpu.VMEM((CHIPS, ROWS, K), jnp.bfloat16),
            dma((4,)),
            dma((SLABS,)),
            dma((SLABS,)),
            dma((len(NEAR),)),
            dma((len(NEAR),)),
            dma((2,)),
            dma((2,)),
            dma((1,)),
            dma((1,)),
            pltpu.SemaphoreType.REGULAR,
            pltpu.SemaphoreType.REGULAR((2,)),
            dma((EXPERTS,)),
            dma((CHIPS,)),
            dma((len(BACK_RELAYED),)),
            dma((len(BACK_RELAYED),)),
            dma((2,)),
            dma((3,)),
            dma((3,)),
            dma((CHIPS,)),
            dma((EXPERTS,)),
            dma((len(BACK_RELAYED),)),
            dma((len(BACK_RELAYED),)),
        ],
        compiler_params=pltpu.CompilerParams(
            collective_id=0, has_side_effects=True, vmem_limit_bytes=48 * 1024 * 1024
        ),
        name="muon_step",
    )(grad_slot, grads, momentum))


def solution(mesh):
    in_specs = (P("group", "slab", None), P("group", None), P("group", "slab", None))
    out_specs = (P("group", "slab", None), P("group", "slab", None))
    return jax.shard_map(
        on_device, mesh=mesh, in_specs=in_specs, out_specs=out_specs, check_vma=False
    )
```

```python
import jax
import jax.numpy as jnp
from jax import lax
from jax.experimental import pallas as pl
from jax.experimental.pallas import tpu as pltpu
from jax.sharding import PartitionSpec as P

MESH = pl.DeviceIdType.MESH

SIDE = 4
CORES = 2
SLABS = SIDE * SIDE * CORES
CHIPS = SIDE * SIDE
GROUPS = 32
EXPERTS = 8
ROWS = 64
M = SLABS * ROWS
K = 512
HALF = K // 2
OWN = CHIPS * ROWS
REACH = 4

COEF_A = 3.4445
COEF_B = -4.775
COEF_C = 2.0315
DECAY_RATE = 0.95
ENTRIES = GROUPS * EXPERTS * M * K

COLUMNS = (2, 1, 3, 0)
BACK_RELAYED = ((2, 1), (2, 3), (1, 1), (3, 3))
ORDER = tuple((hops_x, hops_y) for hops_x in COLUMNS for hops_y in COLUMNS)
AROUND = tuple(
    sorted(
        (
            (hops_x, hops_y, other)
            for hops_x in range(SIDE)
            for hops_y in range(SIDE)
            for other in range(CORES)
            if (hops_x, hops_y, other) != (0, 0, 0)
        ),
        key=lambda h: -min(h[0], SIDE - h[0]) - min(h[1], SIDE - h[1]),
    )
)
GREETED = tuple(off for off in range(-REACH, REACH + 1) if off != 0)
NEAR = tuple(sorted((off for off in range(-2 * REACH, 2 * REACH) if off != 0), key=lambda o: -abs(o)))


def squares(block):
    wide = block.astype(jnp.float32)
    return jnp.sum((wide * wide).reshape(ROWS // 8, 8, K), axis=0)


def fresh(moment, gradient, factor):
    return (
        DECAY_RATE * moment.astype(jnp.float32) + factor * gradient.astype(jnp.float32)
    ).astype(jnp.bfloat16)


def dot(left, right):
    return jnp.dot(left, right, preferred_element_type=jnp.float32)


def kernel(
    slot_hbm,
    grads_hbm,
    momentum_hbm,
    new_ref,
    update_ref,
    slot_ref,
    grads_in,
    pair,
    raw,
    relayed,
    back_relayed,
    fresh_out,
    own_new,
    part,
    slab_parts,
    plane,
    near_parts,
    window,
    far_parts,
    gram_own,
    gram_other,
    current,
    rounded,
    poly_first,
    halfway,
    poly_second,
    scaled,
    outgoing,
    load_sem,
    slab_send,
    slab_recv,
    near_send,
    near_recv,
    far_send,
    far_recv,
    greeting,
    passed,
    raw_send,
    raw_recv,
    relay_send,
    relay_recv,
    local_sem,
    gram_send,
    gram_recv,
    back_send,
    back_recv,
    back_relay_send,
    back_relay_recv,
):
    slab = lax.axis_index("slab")
    group = lax.axis_index("group")
    chip = slab // CORES
    core = slab % CORES
    x = chip // SIDE
    y = chip % SIDE
    active = (x + y) % 2 == 0
    mine = x * 2 + y // 2

    def along_slab(other):
        return (other, group)

    def device_of(at_x, at_y):
        return (at_x * SIDE + at_y) * CORES + core

    def around(hops):
        hops_x, hops_y, other = hops
        return ((x + hops_x) % SIDE * SIDE + (y + hops_y) % SIDE) * CORES + (core + other) % CORES

    def along_group(offset):
        return (slab, (group + offset + GROUPS) % GROUPS)

    def send(src, dst, send_sem, recv_sem, device):
        return pltpu.make_async_remote_copy(
            src_ref=src,
            dst_ref=dst,
            send_sem=send_sem,
            recv_sem=recv_sem,
            device_id=device,
            device_id_type=MESH,
        )

    load_grads = pltpu.make_async_copy(grads_hbm, grads_in, load_sem.at[0])
    load_momentum = pltpu.make_async_copy(momentum_hbm, pair.at[:, 0], load_sem.at[1])
    load_slots = pltpu.make_async_copy(slot_hbm, slot_ref, load_sem.at[2])
    load_slots.start()
    load_grads.start()
    load_momentum.start()

    along = core == 1
    unseen = jnp.maximum(REACH - group, 0)
    barrier = pltpu.get_barrier_semaphore()

    @pl.when(along)
    def _():
        for offset in GREETED:

            @pl.when(group + offset < GROUPS)
            def _():
                pl.semaphore_signal(
                    barrier, inc=1, device_id=along_group(offset), device_id_type=MESH
                )

    for hops in AROUND:
        pl.semaphore_signal(
            barrier, inc=1, device_id=along_slab(around(hops)), device_id_type=MESH
        )

    load_slots.wait()
    load_grads.wait()
    total = jnp.zeros((8, K), jnp.float32)
    for expert in range(EXPERTS):
        block = grads_in[slot_ref[0, expert]]
        pair[expert, 1] = block
        total += squares(block)
    lanes = total[:, :128] + total[:, 128:256] + total[:, 256:384] + total[:, 384:]
    part[...] = jnp.sum(lanes, axis=0, keepdims=True)
    load_momentum.wait()
    pl.semaphore_wait(barrier, SLABS - 1 + core * (len(GREETED) - unseen))

    slab_copies = [
        send(
            part,
            slab_parts.at[index],
            slab_send.at[index],
            slab_recv.at[index],
            along_slab(around(hops)),
        )
        for index, hops in enumerate(AROUND)
    ]
    for copy in slab_copies:
        copy.start()

    def pass_on():
        for side, offset in enumerate((REACH, -REACH)):
            pl.semaphore_signal(
                passed.at[side], inc=1, device_id=along_group(offset), device_id_type=MESH
            )

    @pl.when(along)
    def _():
        for offset in range(1, REACH + 1):

            @pl.when(group + offset >= GROUPS)
            def _():
                pl.semaphore_signal(
                    greeting, inc=1, device_id=along_group(offset), device_id_type=MESH
                )

        @pl.when(unseen == 0)
        def _():
            pass_on()

    def raw_route(hops, which):
        column = (x + hops) % SIDE
        row = which * 2 + column % 2
        return (
            column * 2 + which,
            column,
            row,
            (SIDE - hops) % SIDE,
            (y + SIDE - row) % SIDE,
            COLUMNS.index(hops) * 2 + which,
        )

    def raw_direct(hops, which):
        expert, column, row, from_x, from_y, index = raw_route(hops, which)
        place = from_x * SIDE + from_y
        return send(
            pair.at[expert],
            raw.at[place],
            raw_send.at[index],
            raw_recv.at[place],
            along_slab(device_of(column, row)),
        )

    def raw_relayed(hops, which, slot, by_x, by_y):
        expert, column, row, from_x, from_y, index = raw_route(hops, which)
        return send(
            pair.at[expert],
            relayed.at[slot],
            raw_send.at[index],
            relay_recv.at[slot],
            along_slab(device_of((column + by_x) % SIDE, (row + by_y) % SIDE)),
        )

    def relay_forward(slot):
        if slot < 2:
            towards = (x, (y + 1 + 2 * (y % 2)) % SIDE)
            place = (1 + 2 * slot) * SIDE + 2
        else:
            towards = ((x + (3 if slot == 2 else 1)) % SIDE, y)
            place = 5 if slot == 2 else 15
        return send(
            relayed.at[slot],
            raw.at[place],
            relay_send.at[slot],
            raw_recv.at[place],
            along_slab(device_of(*towards)),
        )

    def relay_wait(slot):
        send(
            pair.at[0], relayed.at[slot], raw_send.at[0], relay_recv.at[slot], along_slab(slab)
        ).wait_recv()

    def relay(slots):
        @pl.when(jnp.logical_not(active))
        def _():
            for slot in slots:
                relay_wait(slot)
                relay_forward(slot).start()

    local_copy = pltpu.make_async_copy(pair.at[mine], raw.at[0], local_sem.at[0])

    for copy in slab_copies:
        copy.wait_recv()

    plane[...] = part[...] + jnp.sum(slab_parts[...], axis=0)

    near_copies = [
        send(
            plane,
            near_parts.at[index],
            near_send.at[index],
            near_recv.at[index],
            along_group(offset),
        )
        for index, offset in enumerate(NEAR)
    ]

    far_copies = [
        send(
            window,
            far_parts.at[side],
            far_send.at[receiver, side],
            far_recv.at[side],
            (chip * CORES + receiver, (group + offset + GROUPS) % GROUPS),
        )
        for receiver in range(CORES)
        for side, offset in enumerate((2 * REACH, -2 * REACH))
    ]

    def start_near():
        for side in range(2):
            pl.semaphore_wait(passed.at[side], 1)
        for copy in near_copies:
            copy.start()

    @pl.when(jnp.logical_and(along, unseen == 0))
    def _():
        start_near()

    for hops, diagonal in ((1, 3), (3, 1)):
        for which in range(2):
            from_y = raw_route(hops, which)[4]
            row = raw_route(hops, which)[2]

            @pl.when(from_y == diagonal)
            def _():
                raw_relayed(hops, which, 2 if diagonal == 1 else 3, SIDE - hops, 0).start()

            @pl.when(from_y == 2)
            def _():
                raw_relayed(
                    hops, which, 1 if diagonal == 3 else 0, 0, 1 + 2 * (row % 2)
                ).start()

    for hops in COLUMNS:
        for which in range(2):
            from_y = raw_route(hops, which)[4]
            if hops == 0:
                direct = from_y != 0
            elif hops == 2:
                direct = True
            else:
                direct = jnp.logical_and(from_y != 2, from_y != SIDE - hops)

            @pl.when(direct)
            def _():
                raw_direct(hops, which).start()

    @pl.when(active)
    def _():
        local_copy.start()

    @pl.when(jnp.logical_and(along, unseen > 0))
    def _():
        pl.semaphore_wait(greeting, unseen)
        pass_on()
        start_near()

    @pl.when(along)
    def _():
        for copy in near_copies:
            copy.wait_recv()
        window[...] = plane[...] + jnp.sum(near_parts[...], axis=0)
        for copy in far_copies:
            copy.start()
        relay((2, 3, 0, 1))

    @pl.when(jnp.logical_not(along))
    def _():
        relay((2, 3, 0, 1))

    for copy in far_copies[:2]:
        copy.wait_recv()

    total_sq = jnp.sum(jnp.sum(far_parts[...], axis=0), axis=1, keepdims=True)
    root_mean = jnp.sqrt(total_sq / ENTRIES + 1e-06)
    factor = jnp.minimum(1.0, 1.0 / root_mean)

    def own_result():
        for expert in range(EXPERTS):
            fresh_out[expert] = fresh(pair[expert, 0], pair[expert, 1], factor)

    def gram_copies():
        partner = along_slab(chip * CORES + 1 - core)
        return [
            send(
                gram_own.at[index],
                gram_other.at[index],
                gram_send.at[index],
                gram_recv.at[index],
                partner,
            )
            for index in range(3)
        ]

    def back_copy(hops):
        hops_x, hops_y = hops
        place = ORDER.index(hops)
        if (hops_x, hops_y) in BACK_RELAYED:
            slot = BACK_RELAYED.index((hops_x, hops_y))
            if slot < 2:
                by = ((x + 3 + 2 * (x % 2)) % SIDE, y)
            else:
                by = (x, (y + hops_y) % SIDE)
            return send(
                outgoing.at[place],
                back_relayed.at[slot],
                back_send.at[place],
                back_relay_recv.at[slot],
                along_slab(device_of(*by)),
            )
        target = device_of((x + hops_x) % SIDE, (y + hops_y) % SIDE)
        return send(
            outgoing.at[place],
            update_ref.at[mine],
            back_send.at[place],
            back_recv.at[mine],
            along_slab(target),
        )

    def back_forward(slot):
        hops_x, hops_y = BACK_RELAYED[slot]
        if slot < 2:
            of_x, of_y = (x + 3 + 2 * (x % 2)) % SIDE, y
        else:
            of_x, of_y = x, (y + SIDE - hops_y) % SIDE
        expert = of_x * 2 + of_y // 2
        return send(
            back_relayed.at[slot],
            update_ref.at[expert],
            back_relay_send.at[slot],
            back_recv.at[expert],
            along_slab(device_of((of_x + hops_x) % SIDE, (of_y + hops_y) % SIDE)),
        )

    def back_wait(slot):
        send(
            outgoing.at[0],
            back_relayed.at[slot],
            back_send.at[0],
            back_relay_recv.at[slot],
            along_slab(slab),
        ).wait_recv()

    @pl.when(active)
    def _():
        local_copy.wait()

        for place in range(CHIPS):
            if place > 0:
                send(
                    pair.at[0], raw.at[place], raw_send.at[0], raw_recv.at[place], along_slab(slab)
                ).wait_recv()
            row = ORDER.index((place // SIDE, place % SIDE)) * ROWS
            own_new[row : row + ROWS, :] = fresh(
                raw[place, 0], raw[place, 1], factor
            )

        for index, (left, right) in enumerate(((0, 0), (0, 1), (1, 1))):
            gram_own[index] = lax.dot_general(
                own_new[:, left * HALF : (left + 1) * HALF],
                own_new[:, right * HALF : (right + 1) * HALF],
                (((0,), (0,)), ((), ())),
                preferred_element_type=jnp.float32,
            )
            if index > 0:
                gram_copies()[index - 1].start()
        gram_copies()[2].start()
        for copy in gram_copies():
            copy.wait_recv()

        trace = jnp.zeros((128, 128), jnp.float32)
        for index in (0, 2):
            whole = gram_own[index] + gram_other[index]
            gram_own_low, gram_own_high = whole[:128, :128], whole[128:, 128:]
            trace += gram_own_low + gram_own_high
        eye = lax.broadcasted_iota(jnp.int32, (128, 128), 0) == lax.broadcasted_iota(
            jnp.int32, (128, 128), 1
        )
        trace = jnp.where(eye, trace, 0.0)
        frobenius = (
            jnp.sum(jnp.sum(trace, axis=0, keepdims=True), axis=1, keepdims=True) + 1e-06
        )
        inverse = 1.0 / frobenius
        for index, (left, right) in enumerate(((0, 0), (0, 1), (1, 1))):
            block = (gram_own[index] + gram_other[index]) * inverse
            current[left * HALF : (left + 1) * HALF, right * HALF : (right + 1) * HALF] = block
            rounded[left * HALF : (left + 1) * HALF, right * HALF : (right + 1) * HALF] = (
                block.astype(jnp.bfloat16)
            )
            if index == 1:
                block = block.T
                current[HALF:, :HALF] = block
                rounded[HALF:, :HALF] = block.astype(jnp.bfloat16)

        def polynomial(into, start):
            rows = slice(start, start + HALF)
            squared = dot(rounded[rows, :], rounded[...])
            diagonal = lax.broadcasted_iota(jnp.int32, (HALF, K), 0) + start
            identity = jnp.where(
                diagonal == lax.broadcasted_iota(jnp.int32, (HALF, K), 1), COEF_A, 0.0
            )
            into[rows, :] = (identity + COEF_B * current[rows, :] + COEF_C * squared).astype(
                jnp.bfloat16
            )

        halves = (0, HALF)
        for start in halves:
            polynomial(poly_first, start)
        for start in halves:
            rows = slice(start, start + HALF)
            halfway[rows, :] = dot(rounded[rows, :], poly_first[...]).astype(jnp.bfloat16)
        for start in halves:
            rows = slice(start, start + HALF)
            following = dot(poly_first[rows, :], halfway[...])
            current[rows, :] = following
            rounded[rows, :] = following.astype(jnp.bfloat16)
        for start in halves:
            polynomial(poly_second, start)
        root = 1.0 / jnp.sqrt(frobenius)
        for start in halves:
            rows = slice(start, start + HALF)
            scaled[rows, :] = (dot(poly_first[rows, :], poly_second[...]) * root).astype(
                jnp.bfloat16
            )

        for turn in range(SIDE):
            start = turn * SIDE * ROWS
            result = jnp.sqrt(jnp.float32(M)) * dot(
                own_new[start : start + SIDE * ROWS, :], scaled[...]
            )
            outgoing[turn * SIDE : (turn + 1) * SIDE] = result.astype(jnp.bfloat16).reshape(
                SIDE, ROWS, K
            )
            if turn > 0:
                for hops in ORDER[(turn - 1) * SIDE : turn * SIDE]:
                    back_copy(hops).start()
        for hops in ORDER[(SIDE - 1) * SIDE : -1]:
            back_copy(hops).start()
        pltpu.make_async_copy(outgoing.at[CHIPS - 1], update_ref.at[mine], local_sem.at[1]).start()

    own_result()
    new_copy = pltpu.make_async_copy(fresh_out, new_ref, load_sem.at[3])
    new_copy.start()

    @pl.when(jnp.logical_not(active))
    def _():
        for slot in range(len(BACK_RELAYED)):
            back_wait(slot)
            back_forward(slot).start()

    for hops in COLUMNS:
        for which in range(2):
            expert, column, row, from_x, from_y, index = raw_route(hops, which)

            @pl.when(device_of(column, row) != slab)
            def _():
                raw_direct(hops, which).wait_send()
                send(
                    outgoing.at[0],
                    update_ref.at[expert],
                    back_send.at[0],
                    back_recv.at[expert],
                    along_slab(slab),
                ).wait_recv()

    @pl.when(jnp.logical_not(active))
    def _():
        for slot in range(len(BACK_RELAYED)):
            relay_forward(slot).wait_send()
            back_forward(slot).wait_send()

    new_copy.wait()

    @pl.when(active)
    def _():
        pltpu.make_async_copy(outgoing.at[CHIPS - 1], update_ref.at[mine], local_sem.at[1]).wait()
        for copy in gram_copies():
            copy.wait_send()
        for hops in ORDER[:-1]:
            back_copy(hops).wait_send()

    for copy in slab_copies:
        copy.wait_send()

    @pl.when(along)
    def _():
        for copy in near_copies + far_copies:
            copy.wait_send()


def finish_kernel(new_ref, update_ref, new_out, update_out, sem):
    copies = [
        pltpu.make_async_copy(src.at[expert], dst.at[expert], sem.at[which, expert])
        for which, (src, dst) in enumerate(((new_ref, new_out), (update_ref, update_out)))
        for expert in range(EXPERTS)
    ]
    for copy in copies:
        copy.start()
    for copy in copies:
        copy.wait()


def finish(new, update):
    anywhere = (pl.BlockSpec(memory_space=pl.ANY),) * 2
    return pl.pallas_call(
        finish_kernel,
        out_shape=tuple(jax.ShapeDtypeStruct(a.shape, a.dtype) for a in (new, update)),
        in_specs=anywhere,
        out_specs=anywhere,
        scratch_shapes=[pltpu.SemaphoreType.DMA((2, EXPERTS))],
        compiler_params=pltpu.CompilerParams(vmem_limit_bytes=1024 * 1024),
        name="finish",
    )(new, update)


def on_device(grads, grad_slot, momentum):
    shape = pltpu.VMEM(grads.shape, jnp.bfloat16)
    grads, grad_slot, momentum = (
        pltpu.with_memory_space_constraint(a, pltpu.HBM) for a in (grads, grad_slot, momentum)
    )
    scalar = (1, 128)
    dma = pltpu.SemaphoreType.DMA
    return finish(*pl.pallas_call(
        kernel,
        out_shape=(shape, shape),
        in_specs=[
            pl.BlockSpec(memory_space=pltpu.HBM),
            pl.BlockSpec(memory_space=pltpu.HBM),
            pl.BlockSpec(memory_space=pltpu.HBM),
        ],
        out_specs=(pl.BlockSpec(memory_space=pl.ANY),) * 2,
        scratch_shapes=[
            pltpu.SMEM((1, EXPERTS), jnp.int32),
            pltpu.VMEM((EXPERTS, ROWS, K), jnp.bfloat16),
            pltpu.VMEM((EXPERTS, 2, ROWS, K), jnp.bfloat16),
            pltpu.VMEM((CHIPS, 2, ROWS, K), jnp.bfloat16),
            pltpu.VMEM((len(BACK_RELAYED), 2, ROWS, K), jnp.bfloat16),
            pltpu.VMEM((len(BACK_RELAYED), ROWS, K), jnp.bfloat16),
            pltpu.VMEM((EXPERTS, ROWS, K), jnp.bfloat16),
            pltpu.VMEM((OWN, K), jnp.bfloat16),
            pltpu.VMEM(scalar, jnp.float32),
            pltpu.VMEM((SLABS - 1, *scalar), jnp.float32),
            pltpu.VMEM(scalar, jnp.float32),
            pltpu.VMEM((len(NEAR), *scalar), jnp.float32),
            pltpu.VMEM(scalar, jnp.float32),
            pltpu.VMEM((2, *scalar), jnp.float32),
            pltpu.VMEM((3, HALF, HALF), jnp.float32),
            pltpu.VMEM((3, HALF, HALF), jnp.float32),
            pltpu.VMEM((K, K), jnp.float32),
            pltpu.VMEM((K, K), jnp.bfloat16),
            pltpu.VMEM((K, K), jnp.bfloat16),
            pltpu.VMEM((K, K), jnp.bfloat16),
            pltpu.VMEM((K, K), jnp.bfloat16),
            pltpu.VMEM((K, K), jnp.bfloat16),
            pltpu.VMEM((CHIPS, ROWS, K), jnp.bfloat16),
            dma((4,)),
            dma((SLABS,)),
            dma((SLABS,)),
            dma((len(NEAR),)),
            dma((len(NEAR),)),
            dma((2, 2)),
            dma((2,)),
            pltpu.SemaphoreType.REGULAR,
            pltpu.SemaphoreType.REGULAR((2,)),
            dma((EXPERTS,)),
            dma((CHIPS,)),
            dma((len(BACK_RELAYED),)),
            dma((len(BACK_RELAYED),)),
            dma((2,)),
            dma((3,)),
            dma((3,)),
            dma((CHIPS,)),
            dma((EXPERTS,)),
            dma((len(BACK_RELAYED),)),
            dma((len(BACK_RELAYED),)),
        ],
        compiler_params=pltpu.CompilerParams(
            collective_id=0, has_side_effects=True, vmem_limit_bytes=48 * 1024 * 1024
        ),
        name="muon_step",
    )(grad_slot, grads, momentum))


def solution(mesh):
    in_specs = (P("group", "slab", None), P("group", None), P("group", "slab", None))
    out_specs = (P("group", "slab", None), P("group", "slab", None))
    return jax.shard_map(
        on_device, mesh=mesh, in_specs=in_specs, out_specs=out_specs, check_vma=False
    )
```

```python
import jax
import jax.numpy as jnp
from jax import lax
from jax.experimental import pallas as pl
from jax.experimental.pallas import tpu as pltpu
from jax.sharding import PartitionSpec as P

MESH = pl.DeviceIdType.MESH

SIDE = 4
CORES = 2
SLABS = SIDE * SIDE * CORES
CHIPS = SIDE * SIDE
GROUPS = 32
EXPERTS = 8
ROWS = 64
M = SLABS * ROWS
K = 512
HALF = K // 2
OWN = CHIPS * ROWS
REACH = 4

COEF_A = 3.4445
COEF_B = -4.775
COEF_C = 2.0315
DECAY_RATE = 0.95
ENTRIES = GROUPS * EXPERTS * M * K

COLUMNS = (2, 1, 3, 0)
BACK_RELAYED = ((2, 1), (2, 3), (1, 1), (3, 3))
ORDER = tuple((hops_x, hops_y) for hops_x in COLUMNS for hops_y in COLUMNS)
AROUND = tuple(
    sorted(
        (
            (hops_x, hops_y, other)
            for hops_x in range(SIDE)
            for hops_y in range(SIDE)
            for other in range(CORES)
            if (hops_x, hops_y, other) != (0, 0, 0)
        ),
        key=lambda h: -min(h[0], SIDE - h[0]) - min(h[1], SIDE - h[1]),
    )
)
BLOCKS = ((0, 0), (1, 1), (0, 1))
GREETED = tuple(off for off in range(-REACH, REACH + 1) if off != 0)
NEAR = tuple(sorted((off for off in range(-2 * REACH, 2 * REACH) if off != 0), key=lambda o: -abs(o)))


def squares(block):
    wide = block.astype(jnp.float32)
    return jnp.sum((wide * wide).reshape(ROWS // 8, 8, K), axis=0)


def fresh(moment, gradient, factor):
    return (
        DECAY_RATE * moment.astype(jnp.float32) + factor * gradient.astype(jnp.float32)
    ).astype(jnp.bfloat16)


def dot(left, right):
    return jnp.dot(left, right, preferred_element_type=jnp.float32)


def kernel(
    slot_hbm,
    grads_hbm,
    momentum_hbm,
    new_ref,
    update_ref,
    slot_ref,
    grads_in,
    pair,
    raw,
    relayed,
    back_relayed,
    fresh_out,
    own_new,
    part,
    slab_parts,
    plane,
    near_parts,
    window,
    far_parts,
    gram_own,
    gram_other,
    current,
    rounded,
    poly_first,
    halfway,
    poly_second,
    scaled,
    outgoing,
    load_sem,
    slab_send,
    slab_recv,
    near_send,
    near_recv,
    far_send,
    far_recv,
    greeting,
    passed,
    raw_send,
    raw_recv,
    relay_send,
    relay_recv,
    local_sem,
    gram_send,
    gram_recv,
    back_send,
    back_recv,
    back_relay_send,
    back_relay_recv,
):
    slab = lax.axis_index("slab")
    group = lax.axis_index("group")
    chip = slab // CORES
    core = slab % CORES
    x = chip // SIDE
    y = chip % SIDE
    active = (x + y) % 2 == 0
    mine = x * 2 + y // 2

    def along_slab(other):
        return (other, group)

    def device_of(at_x, at_y):
        return (at_x * SIDE + at_y) * CORES + core

    def around(hops):
        hops_x, hops_y, other = hops
        return ((x + hops_x) % SIDE * SIDE + (y + hops_y) % SIDE) * CORES + (core + other) % CORES

    def along_group(offset):
        return (slab, (group + offset + GROUPS) % GROUPS)

    def send(src, dst, send_sem, recv_sem, device):
        return pltpu.make_async_remote_copy(
            src_ref=src,
            dst_ref=dst,
            send_sem=send_sem,
            recv_sem=recv_sem,
            device_id=device,
            device_id_type=MESH,
        )

    load_grads = pltpu.make_async_copy(grads_hbm, grads_in, load_sem.at[0])
    load_momentum = pltpu.make_async_copy(momentum_hbm, pair.at[:, 0], load_sem.at[1])
    load_slots = pltpu.make_async_copy(slot_hbm, slot_ref, load_sem.at[2])
    load_slots.start()
    load_grads.start()
    load_momentum.start()

    along = core == 1
    unseen = jnp.maximum(REACH - group, 0)
    barrier = pltpu.get_barrier_semaphore()

    @pl.when(along)
    def _():
        for offset in GREETED:

            @pl.when(group + offset < GROUPS)
            def _():
                pl.semaphore_signal(
                    barrier, inc=1, device_id=along_group(offset), device_id_type=MESH
                )

    for hops in AROUND:
        pl.semaphore_signal(
            barrier, inc=1, device_id=along_slab(around(hops)), device_id_type=MESH
        )

    load_slots.wait()
    load_grads.wait()
    total = jnp.zeros((8, K), jnp.float32)
    for expert in range(EXPERTS):
        block = grads_in[slot_ref[0, expert]]
        pair[expert, 1] = block
        total += squares(block)
    lanes = total[:, :128] + total[:, 128:256] + total[:, 256:384] + total[:, 384:]
    part[...] = jnp.sum(lanes, axis=0, keepdims=True)
    load_momentum.wait()
    pl.semaphore_wait(barrier, SLABS - 1 + core * (len(GREETED) - unseen))

    slab_copies = [
        send(
            part,
            slab_parts.at[index],
            slab_send.at[index],
            slab_recv.at[index],
            along_slab(around(hops)),
        )
        for index, hops in enumerate(AROUND)
    ]
    for copy in slab_copies:
        copy.start()

    def pass_on():
        for side, offset in enumerate((REACH, -REACH)):
            pl.semaphore_signal(
                passed.at[side], inc=1, device_id=along_group(offset), device_id_type=MESH
            )

    @pl.when(along)
    def _():
        for offset in range(1, REACH + 1):

            @pl.when(group + offset >= GROUPS)
            def _():
                pl.semaphore_signal(
                    greeting, inc=1, device_id=along_group(offset), device_id_type=MESH
                )

        @pl.when(unseen == 0)
        def _():
            pass_on()

    def raw_route(hops, which):
        column = (x + hops) % SIDE
        row = which * 2 + column % 2
        return (
            column * 2 + which,
            column,
            row,
            (SIDE - hops) % SIDE,
            (y + SIDE - row) % SIDE,
            COLUMNS.index(hops) * 2 + which,
        )

    def raw_direct(hops, which):
        expert, column, row, from_x, from_y, index = raw_route(hops, which)
        place = from_x * SIDE + from_y
        return send(
            pair.at[expert],
            raw.at[place],
            raw_send.at[index],
            raw_recv.at[place],
            along_slab(device_of(column, row)),
        )

    def raw_relayed(hops, which, slot, by_x, by_y):
        expert, column, row, from_x, from_y, index = raw_route(hops, which)
        return send(
            pair.at[expert],
            relayed.at[slot],
            raw_send.at[index],
            relay_recv.at[slot],
            along_slab(device_of((column + by_x) % SIDE, (row + by_y) % SIDE)),
        )

    def relay_forward(slot):
        if slot < 2:
            towards = (x, (y + 1 + 2 * (y % 2)) % SIDE)
            place = (1 + 2 * slot) * SIDE + 2
        else:
            towards = ((x + (3 if slot == 2 else 1)) % SIDE, y)
            place = 5 if slot == 2 else 15
        return send(
            relayed.at[slot],
            raw.at[place],
            relay_send.at[slot],
            raw_recv.at[place],
            along_slab(device_of(*towards)),
        )

    def relay_wait(slot):
        send(
            pair.at[0], relayed.at[slot], raw_send.at[0], relay_recv.at[slot], along_slab(slab)
        ).wait_recv()

    def relay(slots):
        @pl.when(jnp.logical_not(active))
        def _():
            for slot in slots:
                relay_wait(slot)
                relay_forward(slot).start()

    local_copy = pltpu.make_async_copy(pair.at[mine], raw.at[0], local_sem.at[0])

    for copy in slab_copies:
        copy.wait_recv()

    plane[...] = part[...] + jnp.sum(slab_parts[...], axis=0)

    near_copies = [
        send(
            plane,
            near_parts.at[index],
            near_send.at[index],
            near_recv.at[index],
            along_group(offset),
        )
        for index, offset in enumerate(NEAR)
    ]

    far_copies = [
        send(
            window,
            far_parts.at[side],
            far_send.at[receiver, side],
            far_recv.at[side],
            (chip * CORES + receiver, (group + offset + GROUPS) % GROUPS),
        )
        for receiver in range(CORES)
        for side, offset in enumerate((2 * REACH, -2 * REACH))
    ]

    def start_near():
        for side in range(2):
            pl.semaphore_wait(passed.at[side], 1)
        for copy in near_copies:
            copy.start()

    @pl.when(jnp.logical_and(along, unseen == 0))
    def _():
        start_near()

    for hops, diagonal in ((1, 3), (3, 1)):
        for which in range(2):
            from_y = raw_route(hops, which)[4]
            row = raw_route(hops, which)[2]

            @pl.when(from_y == diagonal)
            def _():
                raw_relayed(hops, which, 2 if diagonal == 1 else 3, SIDE - hops, 0).start()

            @pl.when(from_y == 2)
            def _():
                raw_relayed(
                    hops, which, 1 if diagonal == 3 else 0, 0, 1 + 2 * (row % 2)
                ).start()

    for hops in COLUMNS:
        for which in range(2):
            from_y = raw_route(hops, which)[4]
            if hops == 0:
                direct = from_y != 0
            elif hops == 2:
                direct = True
            else:
                direct = jnp.logical_and(from_y != 2, from_y != SIDE - hops)

            @pl.when(direct)
            def _():
                raw_direct(hops, which).start()

    @pl.when(active)
    def _():
        local_copy.start()

    @pl.when(jnp.logical_and(along, unseen > 0))
    def _():
        pl.semaphore_wait(greeting, unseen)
        pass_on()
        start_near()

    @pl.when(along)
    def _():
        for copy in near_copies:
            copy.wait_recv()
        window[...] = plane[...] + jnp.sum(near_parts[...], axis=0)
        for copy in far_copies:
            copy.start()
        relay((2, 3, 0, 1))

    @pl.when(jnp.logical_not(along))
    def _():
        relay((2, 3, 0, 1))

    for copy in far_copies[:2]:
        copy.wait_recv()

    total_sq = jnp.sum(jnp.sum(far_parts[...], axis=0), axis=1, keepdims=True)
    root_mean = jnp.sqrt(total_sq / ENTRIES + 1e-06)
    factor = jnp.minimum(1.0, 1.0 / root_mean)

    def own_result():
        for expert in range(EXPERTS):
            fresh_out[expert] = fresh(pair[expert, 0], pair[expert, 1], factor)

    def gram_copies():
        partner = along_slab(chip * CORES + 1 - core)
        return [
            send(
                gram_own.at[index],
                gram_other.at[index],
                gram_send.at[index],
                gram_recv.at[index],
                partner,
            )
            for index in range(3)
        ]

    def back_copy(hops):
        hops_x, hops_y = hops
        place = ORDER.index(hops)
        if (hops_x, hops_y) in BACK_RELAYED:
            slot = BACK_RELAYED.index((hops_x, hops_y))
            if slot < 2:
                by = ((x + 3 + 2 * (x % 2)) % SIDE, y)
            else:
                by = (x, (y + hops_y) % SIDE)
            return send(
                outgoing.at[place],
                back_relayed.at[slot],
                back_send.at[place],
                back_relay_recv.at[slot],
                along_slab(device_of(*by)),
            )
        target = device_of((x + hops_x) % SIDE, (y + hops_y) % SIDE)
        return send(
            outgoing.at[place],
            update_ref.at[mine],
            back_send.at[place],
            back_recv.at[mine],
            along_slab(target),
        )

    def back_forward(slot):
        hops_x, hops_y = BACK_RELAYED[slot]
        if slot < 2:
            of_x, of_y = (x + 3 + 2 * (x % 2)) % SIDE, y
        else:
            of_x, of_y = x, (y + SIDE - hops_y) % SIDE
        expert = of_x * 2 + of_y // 2
        return send(
            back_relayed.at[slot],
            update_ref.at[expert],
            back_relay_send.at[slot],
            back_recv.at[expert],
            along_slab(device_of((of_x + hops_x) % SIDE, (of_y + hops_y) % SIDE)),
        )

    def back_wait(slot):
        send(
            outgoing.at[0],
            back_relayed.at[slot],
            back_send.at[0],
            back_relay_recv.at[slot],
            along_slab(slab),
        ).wait_recv()

    @pl.when(active)
    def _():
        local_copy.wait()

        for place in range(CHIPS):
            if place > 0:
                send(
                    pair.at[0], raw.at[place], raw_send.at[0], raw_recv.at[place], along_slab(slab)
                ).wait_recv()
            row = ORDER.index((place // SIDE, place % SIDE)) * ROWS
            own_new[row : row + ROWS, :] = fresh(
                raw[place, 0], raw[place, 1], factor
            )

        for index, (left, right) in enumerate(BLOCKS):
            gram_own[index] = lax.dot_general(
                own_new[:, left * HALF : (left + 1) * HALF],
                own_new[:, right * HALF : (right + 1) * HALF],
                (((0,), (0,)), ((), ())),
                preferred_element_type=jnp.float32,
            )
            gram_copies()[index].start()
        for copy in gram_copies()[:2]:
            copy.wait_recv()

        trace = jnp.zeros((128, 128), jnp.float32)
        for index in range(2):
            whole = gram_own[index] + gram_other[index]
            gram_own_low, gram_own_high = whole[:128, :128], whole[128:, 128:]
            trace += gram_own_low + gram_own_high
        eye = lax.broadcasted_iota(jnp.int32, (128, 128), 0) == lax.broadcasted_iota(
            jnp.int32, (128, 128), 1
        )
        trace = jnp.where(eye, trace, 0.0)
        frobenius = (
            jnp.sum(jnp.sum(trace, axis=0, keepdims=True), axis=1, keepdims=True) + 1e-06
        )
        inverse = 1.0 / frobenius
        for index, (left, right) in enumerate(BLOCKS):
            if index == 2:
                gram_copies()[2].wait_recv()
            block = (gram_own[index] + gram_other[index]) * inverse
            current[left * HALF : (left + 1) * HALF, right * HALF : (right + 1) * HALF] = block
            rounded[left * HALF : (left + 1) * HALF, right * HALF : (right + 1) * HALF] = (
                block.astype(jnp.bfloat16)
            )
            if index == 2:
                block = block.T
                current[HALF:, :HALF] = block
                rounded[HALF:, :HALF] = block.astype(jnp.bfloat16)

        def polynomial(into, start):
            rows = slice(start, start + HALF)
            squared = dot(rounded[rows, :], rounded[...])
            diagonal = lax.broadcasted_iota(jnp.int32, (HALF, K), 0) + start
            identity = jnp.where(
                diagonal == lax.broadcasted_iota(jnp.int32, (HALF, K), 1), COEF_A, 0.0
            )
            into[rows, :] = (identity + COEF_B * current[rows, :] + COEF_C * squared).astype(
                jnp.bfloat16
            )

        halves = (0, HALF)
        for start in halves:
            polynomial(poly_first, start)
        for start in halves:
            rows = slice(start, start + HALF)
            halfway[rows, :] = dot(rounded[rows, :], poly_first[...]).astype(jnp.bfloat16)
        for start in halves:
            rows = slice(start, start + HALF)
            following = dot(poly_first[rows, :], halfway[...])
            current[rows, :] = following
            rounded[rows, :] = following.astype(jnp.bfloat16)
        for start in halves:
            polynomial(poly_second, start)
        root = 1.0 / jnp.sqrt(frobenius)
        for start in halves:
            rows = slice(start, start + HALF)
            scaled[rows, :] = (dot(poly_first[rows, :], poly_second[...]) * root).astype(
                jnp.bfloat16
            )

        for turn in range(SIDE):
            start = turn * SIDE * ROWS
            result = jnp.sqrt(jnp.float32(M)) * dot(
                own_new[start : start + SIDE * ROWS, :], scaled[...]
            )
            outgoing[turn * SIDE : (turn + 1) * SIDE] = result.astype(jnp.bfloat16).reshape(
                SIDE, ROWS, K
            )
            if turn > 0:
                for hops in ORDER[(turn - 1) * SIDE : turn * SIDE]:
                    back_copy(hops).start()
        for hops in ORDER[(SIDE - 1) * SIDE : -1]:
            back_copy(hops).start()
        pltpu.make_async_copy(outgoing.at[CHIPS - 1], update_ref.at[mine], local_sem.at[1]).start()

    own_result()
    new_copy = pltpu.make_async_copy(fresh_out, new_ref, load_sem.at[3])
    new_copy.start()

    @pl.when(jnp.logical_not(active))
    def _():
        for slot in range(len(BACK_RELAYED)):
            back_wait(slot)
            back_forward(slot).start()

    for hops in COLUMNS:
        for which in range(2):
            expert, column, row, from_x, from_y, index = raw_route(hops, which)

            @pl.when(device_of(column, row) != slab)
            def _():
                raw_direct(hops, which).wait_send()
                send(
                    outgoing.at[0],
                    update_ref.at[expert],
                    back_send.at[0],
                    back_recv.at[expert],
                    along_slab(slab),
                ).wait_recv()

    @pl.when(jnp.logical_not(active))
    def _():
        for slot in range(len(BACK_RELAYED)):
            relay_forward(slot).wait_send()
            back_forward(slot).wait_send()

    new_copy.wait()

    @pl.when(active)
    def _():
        pltpu.make_async_copy(outgoing.at[CHIPS - 1], update_ref.at[mine], local_sem.at[1]).wait()
        for copy in gram_copies():
            copy.wait_send()
        for hops in ORDER[:-1]:
            back_copy(hops).wait_send()

    for copy in slab_copies:
        copy.wait_send()

    @pl.when(along)
    def _():
        for copy in near_copies + far_copies:
            copy.wait_send()


def finish_kernel(new_ref, update_ref, new_out, update_out, sem):
    copies = [
        pltpu.make_async_copy(src.at[expert], dst.at[expert], sem.at[which, expert])
        for which, (src, dst) in enumerate(((new_ref, new_out), (update_ref, update_out)))
        for expert in range(EXPERTS)
    ]
    for copy in copies:
        copy.start()
    for copy in copies:
        copy.wait()


def finish(new, update):
    anywhere = (pl.BlockSpec(memory_space=pl.ANY),) * 2
    return pl.pallas_call(
        finish_kernel,
        out_shape=tuple(jax.ShapeDtypeStruct(a.shape, a.dtype) for a in (new, update)),
        in_specs=anywhere,
        out_specs=anywhere,
        scratch_shapes=[pltpu.SemaphoreType.DMA((2, EXPERTS))],
        compiler_params=pltpu.CompilerParams(vmem_limit_bytes=1024 * 1024),
        name="finish",
    )(new, update)


def on_device(grads, grad_slot, momentum):
    shape = pltpu.VMEM(grads.shape, jnp.bfloat16)
    grads, grad_slot, momentum = (
        pltpu.with_memory_space_constraint(a, pltpu.HBM) for a in (grads, grad_slot, momentum)
    )
    scalar = (1, 128)
    dma = pltpu.SemaphoreType.DMA
    return finish(*pl.pallas_call(
        kernel,
        out_shape=(shape, shape),
        in_specs=[
            pl.BlockSpec(memory_space=pltpu.HBM),
            pl.BlockSpec(memory_space=pltpu.HBM),
            pl.BlockSpec(memory_space=pltpu.HBM),
        ],
        out_specs=(pl.BlockSpec(memory_space=pl.ANY),) * 2,
        scratch_shapes=[
            pltpu.SMEM((1, EXPERTS), jnp.int32),
            pltpu.VMEM((EXPERTS, ROWS, K), jnp.bfloat16),
            pltpu.VMEM((EXPERTS, 2, ROWS, K), jnp.bfloat16),
            pltpu.VMEM((CHIPS, 2, ROWS, K), jnp.bfloat16),
            pltpu.VMEM((len(BACK_RELAYED), 2, ROWS, K), jnp.bfloat16),
            pltpu.VMEM((len(BACK_RELAYED), ROWS, K), jnp.bfloat16),
            pltpu.VMEM((EXPERTS, ROWS, K), jnp.bfloat16),
            pltpu.VMEM((OWN, K), jnp.bfloat16),
            pltpu.VMEM(scalar, jnp.float32),
            pltpu.VMEM((SLABS - 1, *scalar), jnp.float32),
            pltpu.VMEM(scalar, jnp.float32),
            pltpu.VMEM((len(NEAR), *scalar), jnp.float32),
            pltpu.VMEM(scalar, jnp.float32),
            pltpu.VMEM((2, *scalar), jnp.float32),
            pltpu.VMEM((3, HALF, HALF), jnp.float32),
            pltpu.VMEM((3, HALF, HALF), jnp.float32),
            pltpu.VMEM((K, K), jnp.float32),
            pltpu.VMEM((K, K), jnp.bfloat16),
            pltpu.VMEM((K, K), jnp.bfloat16),
            pltpu.VMEM((K, K), jnp.bfloat16),
            pltpu.VMEM((K, K), jnp.bfloat16),
            pltpu.VMEM((K, K), jnp.bfloat16),
            pltpu.VMEM((CHIPS, ROWS, K), jnp.bfloat16),
            dma((4,)),
            dma((SLABS,)),
            dma((SLABS,)),
            dma((len(NEAR),)),
            dma((len(NEAR),)),
            dma((2, 2)),
            dma((2,)),
            pltpu.SemaphoreType.REGULAR,
            pltpu.SemaphoreType.REGULAR((2,)),
            dma((EXPERTS,)),
            dma((CHIPS,)),
            dma((len(BACK_RELAYED),)),
            dma((len(BACK_RELAYED),)),
            dma((2,)),
            dma((3,)),
            dma((3,)),
            dma((CHIPS,)),
            dma((EXPERTS,)),
            dma((len(BACK_RELAYED),)),
            dma((len(BACK_RELAYED),)),
        ],
        compiler_params=pltpu.CompilerParams(
            collective_id=0, has_side_effects=True, vmem_limit_bytes=48 * 1024 * 1024
        ),
        name="muon_step",
    )(grad_slot, grads, momentum))


def solution(mesh):
    in_specs = (P("group", "slab", None), P("group", None), P("group", "slab", None))
    out_specs = (P("group", "slab", None), P("group", "slab", None))
    return jax.shard_map(
        on_device, mesh=mesh, in_specs=in_specs, out_specs=out_specs, check_vma=False
    )
```
